128 devices in a mesh: gx: 8 (over y, core), gy: 16 (over z, x).
Axes of the slice: x: 4, y: 4, z: 4, core: 2. Of those that a mesh axis runs over, the one named last changes fastest.
Arguments:
- velocity: float32 [3, 768, 512, 256], P(None, 'gx', 'gy'), may hold values from -6 to 6
- inflow: float32 [3, 512, 256], P(None, 'gy'), may hold values from -5 to 5
- positions: int32 [8, 64, 3, 256], P('gx'), may hold values from 0 to 765, as said below
- tiles: int32 [8, 64, 2], P('gx'), may hold values from 0 to 15, as said below
- coefs: float32 [8, 64, 256], P('gx'), may hold values from 2 to 20
- counts: int32 [8], P('gx'), may hold values from 1 to 64, as said below
Outputs:
- velocity_next: float32 [3, 768, 512, 256], P(None, 'gx', 'gy')
- blade_force: float32 [8, 64, 3, 256], P('gx')
The draws below stay inside these ranges and needn't reach their ends.
Inputs may be any that keep to these rules, and one draw needn't show every extreme that they name: `positions`: for a record of tile row r, coordinate 0 is one value for all its points, from r * 96 + 2 to r * 96 + 93; coordinate 2 lies from 2 to 253; the points of a record lie on a straight segment in y and z. tiles[r, s, 1] is 2 or 3; the first listed y tile is the lowest y tile that holds a cell within 2 in y of some point of the record, or the tile after it. Records of row r with index below counts[r] are live; some row is full and some row has one live record.
All inputs are finite; a program needn't handle non-finite values.
Results may differ from the reference program's by a relative error of at most 0.00008.
Values sent between devices are 32-bit elements; how exact they have to be, the bound alone decides.
A program may use at most 128 MiB of HBM per device.

```python
import math
import jax
import jax.numpy as jnp
from jax import lax

CX = 96
CY = 32
NZ = 256
REC_ROW = 64
PTS = 256
RAD = 2
NX = 768
NY = 512
N_GX = 8
N_GY = 16


def blade_layout(key):
    shape = (N_GX, REC_ROW)
    reach = 2 * CY - 2 * RAD
    lift = min(reach, (NZ - 2 * RAD - 2) // 2)
    rows = jnp.arange(N_GX, dtype=jnp.int32)[:, None]
    slots = jnp.arange(REC_ROW, dtype=jnp.int32)[None, :]
    hub_x = rows * CX + jax.random.randint(jax.random.fold_in(key, 31), shape, RAD, CX - RAD)
    hub_x = jnp.where(slots == 0, rows * CX + CX - RAD - 1, hub_x)
    centre = jax.random.randint(jax.random.fold_in(key, 32), (N_GX, 1), 0, NY)
    nearby = centre + jax.random.randint(jax.random.fold_in(key, 33), shape, -2 * CY, 2 * CY)
    anywhere = jax.random.randint(jax.random.fold_in(key, 34), shape, 0, NY)
    chooser = jax.random.randint(jax.random.fold_in(key, 35), shape, 0, 3)
    hub_y = jnp.where(chooser == 0, anywhere, nearby)
    third_tile = (rows * 3 + 1) % N_GY
    hub_y = jnp.where(slots == 0, NY - CY // 2, hub_y)
    hub_y = jnp.where(slots == 1, third_tile * CY + CY - 1 + RAD, hub_y)
    hub_y = jnp.where(slots == 2, RAD, hub_y)
    length = jax.random.randint(jax.random.fold_in(key, 36), shape, reach // 2, reach + 1)
    direction = 2 * jax.random.randint(jax.random.fold_in(key, 37), shape, 0, 2) - 1
    end_y = jnp.where(slots < 3, reach, length * direction)
    end_z = jax.random.randint(jax.random.fold_in(key, 38), shape, -lift, lift + 1)
    hub_z = jax.random.randint(jax.random.fold_in(key, 39), shape, RAD + lift, NZ - RAD - lift)
    along = jnp.arange(PTS, dtype=jnp.int32)
    raw_y = hub_y[:, :, None] + along[None, None, :] * end_y[:, :, None] // PTS
    cell_z = hub_z[:, :, None] + along[None, None, :] * end_z[:, :, None] // PTS
    cell_x = jnp.broadcast_to(hub_x[:, :, None], raw_y.shape)
    positions = jnp.stack([cell_x, raw_y % NY, cell_z], axis=2).astype(jnp.int32)
    low_tile = (jnp.min(raw_y, axis=2) - RAD) // CY
    first_shift = jax.random.randint(jax.random.fold_in(key, 40), shape, 0, 2)
    list_count = jax.random.randint(jax.random.fold_in(key, 41), shape, 2, 4)
    tiles = jnp.stack([(low_tile + first_shift) % N_GY, list_count], axis=2).astype(jnp.int32)
    return (positions, tiles)


def draw_positions(key, part):
    return blade_layout(key)[0]


def draw_tiles(key, part):
    return blade_layout(key)[1]


def draw_counts(key, part):
    key_count = jax.random.fold_in(key, 21)
    key_full = jax.random.fold_in(key, 22)
    drawn = jax.random.randint(key_count, (N_GX,), 1, REC_ROW + 1)
    full_row = jax.random.randint(key_full, (), 0, N_GX)
    row_index = jnp.arange(N_GX, dtype=jnp.int32)
    single = jnp.where(row_index == (full_row + 1) % N_GX, 1, drawn)
    return jnp.where(row_index == full_row, REC_ROW, single).astype(jnp.int32)


def block_scale(stream_key, shape, split, least, largest):
    level = 1.0
    for dim, shards_of in split:
        draws = jax.random.uniform(jax.random.fold_in(jax.random.fold_in(stream_key, 6), dim), (shards_of,), jnp.float32, least / len(split), largest / len(split))
        level = level * jnp.repeat(jnp.exp(draws), shape[dim] // shards_of).reshape((-1,) + (1,) * (len(shape) - 1 - dim))
    return level


def noise(rng, extent, scale, limit, pieces=(), kind=jnp.bfloat16):
    values = scale * jax.random.normal(rng, extent, jnp.float32)
    if pieces:
        values = values * block_scale(rng, extent, pieces, -0.22, 0.18)
    return jnp.clip(values, -limit, limit).astype(kind)


def setup_inputs(seed: int = 0) -> dict:
    seeds = jax.random.split(jax.random.key(seed), 7)
    velocity = noise(seeds[0], (3, NX, NY, NZ), 1.0, 6.0, ((1, 8), (2, 16)), jnp.float32)
    inflow = noise(seeds[1], (3, NY, NZ), 1.0, 5.0, ((1, 16),), jnp.float32)
    positions = draw_positions(jax.random.fold_in(seeds[6], 71), 0)
    tiles = draw_tiles(jax.random.fold_in(seeds[6], 71), 0)
    coefs = jnp.clip(jnp.exp(math.log(20.0) - 2.3025851 * jax.random.uniform(seeds[4], (N_GX, REC_ROW, PTS), jnp.float32) ** block_scale(seeds[4], (N_GX, REC_ROW, PTS), ((0, 8),), -0.2, 0.2)), 2.0, 20.0)
    counts = draw_counts(jax.random.fold_in(seeds[6], 71), 0)
    return {"velocity": velocity, "inflow": inflow, "positions": positions, "tiles": tiles, "coefs": coefs, "counts": counts}


VISCOSITY = 0.05
TIME_STEP = 0.1
WIDTH_EPS = 1.5
ROOT_PI = 1.7724538509055159

def kernel_weight(offset):
    inside = jnp.abs(offset) <= RAD
    dist = offset.astype(jnp.float32)
    value = jnp.exp(-(dist / WIDTH_EPS) ** 2) / (WIDTH_EPS * ROOT_PI)
    return jnp.where(inside, value, jnp.zeros_like(value))

def tendency(field, inflow, force):
    xpad = jnp.concatenate([inflow[:, None], field, field[:, -1:]], axis=1)
    ypad = jnp.concatenate([field[:, :, -1:], field, field[:, :, :1]], axis=2)
    zpad = jnp.pad(field, ((0, 0), (0, 0), (0, 0), (1, 1)))
    east, west = (xpad[:, 2:], xpad[:, :-2])
    north, south = (ypad[:, :, 2:], ypad[:, :, :-2])
    upper, lower = (zpad[:, :, :, 2:], zpad[:, :, :, :-2])
    advect = field[0:1] * (east - west) * 0.5 + field[1:2] * (north - south) * 0.5 + field[2:3] * (upper - lower) * 0.5
    diffuse = east + west + north + south + upper + lower - 6.0 * field
    return -advect + VISCOSITY * diffuse + force

def forcing(field, positions, tiles, coefs, counts):
    window = 2 * RAD + 1
    offsets = jnp.arange(window, dtype=jnp.int32) - RAD
    across = kernel_weight(offsets)
    padded = jnp.concatenate([field[:, :, -RAD:], field, field[:, :, :RAD]], axis=2)
    px = positions[:, :, 0, :].reshape(-1)
    py = positions[:, :, 1, :].reshape(-1)
    pz = positions[:, :, 2, :].reshape(-1)
    point_shape = (N_GX, REC_ROW, PTS)
    first_tile = jnp.broadcast_to(tiles[:, :, 0:1], point_shape).reshape(-1)
    tile_count = jnp.broadcast_to(tiles[:, :, 1:2], point_shape).reshape(-1)
    cell_y = (py[:, None] + offsets[None, :]) % NY
    listed = (cell_y // CY - first_tile[:, None]) % N_GY < tile_count[:, None]
    along_y = across[None, :] * listed.astype(jnp.float32)
    kernel_cube = across[None, :, None, None] * along_y[:, None, :, None] * across[None, None, None, :]

    def sample(xs, ys, zs, weight):
        block = lax.dynamic_slice(padded, (jnp.int32(0), xs - RAD, ys, zs - RAD), (3, window, window, window))
        return lax.optimization_barrier(jnp.sum(block * weight[None], axis=(1, 2, 3)))
    sampled = jax.vmap(sample, out_axes=1)(px, py, pz, kernel_cube)
    live_mask = jnp.arange(REC_ROW, dtype=jnp.int32)[None, :, None] < counts[:, None, None]
    strength = (coefs * live_mask.astype(jnp.float32)).reshape(-1)
    speed_norm = jnp.sqrt(lax.optimization_barrier(jnp.sum(sampled * sampled, axis=0)))
    point_force = -strength * speed_norm * sampled
    ix = px[:, None, None, None] + offsets[None, :, None, None]
    iy = (py[:, None, None, None] + offsets[None, None, :, None]) % NY
    iz = pz[:, None, None, None] + offsets[None, None, None, :]
    values = point_force[:, :, None, None, None] * kernel_cube[None]
    grid_force = jnp.zeros_like(field).at[:, ix, iy, iz].add(values)
    return (grid_force, point_force)

def reference(velocity, inflow, positions, tiles, coefs, counts):
    force_a, points_a = forcing(velocity, positions, tiles, coefs, counts)
    section = velocity + TIME_STEP * tendency(velocity, inflow, force_a)
    force_b, points_b = forcing(section, positions, tiles, coefs, counts)
    velocity_next = 0.5 * (velocity + section + TIME_STEP * tendency(section, inflow, force_b))
    mean_force = 0.5 * (points_a + points_b)
    blade_force = mean_force.reshape(3, N_GX, REC_ROW, PTS).transpose(1, 2, 0, 3)
    return (velocity_next, blade_force)
```

```python
import functools
import math

import jax
import jax.numpy as jnp
from jax import lax
from jax.experimental import pallas as pl
from jax.experimental.pallas import tpu as pltpu
from jax.sharding import PartitionSpec as P

F32, BF16, I32 = jnp.float32, jnp.bfloat16, jnp.int32
RAD = 2
VISCOSITY = 0.05
TIME_STEP = 0.1
WIDTH_EPS = 1.5
K0, K1, K2 = (
    math.exp(-((d / WIDTH_EPS) ** 2)) / (WIDTH_EPS * math.sqrt(math.pi)) for d in range(3)
)
MESH = pl.DeviceIdType.MESH
VMEM = pl.BlockSpec(memory_space=pltpu.VMEM)
SMEM = pl.BlockSpec(memory_space=pltpu.SMEM)
HBM = pl.BlockSpec(memory_space=pltpu.HBM)
LANES = 128
CHUNKS = 4


def params(**kw):
    return pltpu.CompilerParams(vmem_limit_bytes=16 << 20, **kw)


def local_y(pos_y, tile_y, cells_y, total_y):
    return lax.rem(pos_y - tile_y * cells_y + total_y + total_y // 2, total_y) - total_y // 2


def smooth_z(block):
    near = pltpu.roll(block, 1, 1) + pltpu.roll(block, block.shape[1] - 1, 1)
    far = pltpu.roll(block, 2, 1) + pltpu.roll(block, block.shape[1] - 2, 1)
    return K0 * block + K1 * near + K2 * far


def split_dot(block, pick, dims):
    rows = block.shape[0]
    high = block.astype(BF16)
    low = (block - high.astype(F32)).astype(BF16)
    both = lax.dot_general(
        jnp.concatenate([high, low], axis=0), pick, (dims, ((), ())), preferred_element_type=F32
    )
    return both[:rows] + both[rows:]


def point_pick(pos_ref, rec, depth):
    pos_z = pos_ref[2, pl.ds(rec, 1), :]
    cell = lax.broadcasted_iota(I32, (depth, pos_z.shape[1]), 0)
    return (cell == pos_z).astype(F32).astype(BF16)


def weight_y(pos_ref, rec, tile_y, cells_y, total_y):
    here = local_y(pos_ref[1, pl.ds(rec, 1), :], tile_y, cells_y, total_y)
    dist = jnp.abs(lax.broadcasted_iota(I32, (cells_y, here.shape[1]), 0) - here)
    return jnp.where(
        dist == 0, K0, jnp.where(dist == 1, K1, jnp.where(dist == 2, K2, 0.0))
    ).astype(F32)


def sample_record(field, pos_ref, part_ref, rec, hub, tile_y, total_y):
    comps, _, cells_y, depth = field.shape
    planes = (
        K0 * field[:, hub]
        + K1 * (field[:, hub - 1] + field[:, hub + 1])
        + K2 * (field[:, hub - 2] + field[:, hub + 2])
    )
    smooth = smooth_z(planes.reshape(comps * cells_y, depth))
    inner = split_dot(smooth, point_pick(pos_ref, rec, depth), ((1,), (0,)))
    along = weight_y(pos_ref, rec, tile_y, cells_y, total_y)
    value = jnp.sum(inner.reshape(comps, cells_y, -1) * along[None], axis=1)
    group, row = rec // 8, lax.rem(rec, 8)
    for half in range(2):
        for c in range(comps):
            part_ref[half * 8 + group, c, pl.ds(row, 1), :] = value[
                c : c + 1, half * LANES : (half + 1) * LANES
            ]


def spread_record(field, pos_ref, coef_ref, samp_ref, rec, hub, scale, tile_y, total_y):
    comps, _, cells_y, depth = field.shape
    group, row = rec // 8, lax.rem(rec, 8)
    sampled = [
        jnp.concatenate(
            [samp_ref[half * 8 + group, c, pl.ds(row, 1), :] for half in range(2)], axis=1
        )
        for c in range(comps)
    ]
    speed = jnp.sqrt(sampled[0] * sampled[0] + sampled[1] * sampled[1] + sampled[2] * sampled[2])
    strength = coef_ref[pl.ds(rec, 1), :] * speed * (-scale)
    along = weight_y(pos_ref, rec, tile_y, cells_y, total_y)
    weighted = jnp.concatenate([along * (strength * value) for value in sampled], axis=0)
    slab = split_dot(weighted, point_pick(pos_ref, rec, depth), ((1,), (1,)))
    slab = smooth_z(slab).reshape(comps, cells_y, depth)
    for d, weight in ((-2, K2), (-1, K1), (0, K0), (1, K1), (2, K2)):
        field[:, hub + d] += weight * slab


def sample_first(total_y, groups_y, vel_hbm, pos_ref, tiles_ref, counts_ref,
                 field, part_ref, plan_ref, flags, table, sems):
    recs = pos_ref.shape[1]
    cells_x, cells_y = field.shape[1:3]
    tile_x, tile_y = lax.axis_index("gx"), lax.axis_index("gy")
    load = pltpu.make_async_copy(vel_hbm, field, sems.at[0])
    load.start()
    part_ref[...] = jnp.zeros_like(part_ref)
    here = local_y(pos_ref[1], tile_y, cells_y, total_y)
    near = ((here >= -RAD) & (here < cells_y + RAD)).astype(I32)
    touched = jnp.max(near, axis=1, keepdims=True)
    hub = pos_ref[0, :, 0:LANES] - tile_x * cells_x
    flags[...] = jnp.where(touched > 0, hub, -1)
    fetch = pltpu.make_async_copy(flags, table, sems.at[1])
    fetch.start()
    fetch.wait()

    def place(rec, count):
        hub = table[rec, 0]
        listed = lax.rem(tile_y - tiles_ref[0, rec] + groups_y, groups_y) < tiles_ref[1, rec]
        plan_ref[0, count] = rec
        plan_ref[1, count] = hub
        take = listed & (rec < counts_ref[0]) & (hub >= 0)
        return count + take.astype(I32)

    count = lax.fori_loop(0, recs, place, jnp.int32(0))
    plan_ref[0, LANES - 1] = count
    load.wait()

    @pl.loop(0, count)
    def _(n):
        sample_record(field, pos_ref, part_ref, plan_ref[0, n], plan_ref[1, n], tile_y, total_y)


def spread_and_sample(total_y, plan_ref, pos_ref, coef_ref, samp_ref, _, field, part_ref):
    tile_y = lax.axis_index("gy")
    count = plan_ref[0, LANES - 1]
    part_ref[...] = jnp.zeros_like(part_ref)

    @pl.loop(0, count)
    def _(n):
        spread_record(field, pos_ref, coef_ref, samp_ref, plan_ref[0, n], plan_ref[1, n],
                      TIME_STEP, tile_y, total_y)

    @pl.loop(0, count)
    def _(n):
        sample_record(field, pos_ref, part_ref, plan_ref[0, n], plan_ref[1, n], tile_y, total_y)


def spread_last(total_y, plan_ref, pos_ref, coef_ref, counts_ref, samp_a, samp_b, _,
                field, next_hbm, blade_ref, sems):
    tile_y = lax.axis_index("gy")
    comps, recs, _ = blade_ref.shape
    count = plan_ref[0, LANES - 1]

    @pl.loop(0, count)
    def _(n):
        spread_record(field, pos_ref, coef_ref, samp_b, plan_ref[0, n], plan_ref[1, n],
                      0.5 * TIME_STEP, tile_y, total_y)

    store = pltpu.make_async_copy(field, next_hbm, sems.at[0])
    store.start()
    for half in range(2):
        lanes = pl.ds(half * LANES, LANES)
        for group in range(recs // 8):
            rows = pl.ds(group * 8, 8)
            a = [samp_a[half * 8 + group, c] for c in range(comps)]
            b = [samp_b[half * 8 + group, c] for c in range(comps)]
            speed_a = jnp.sqrt(a[0] * a[0] + a[1] * a[1] + a[2] * a[2])
            speed_b = jnp.sqrt(b[0] * b[0] + b[1] * b[1] + b[2] * b[2])
            rec = group * 8 + lax.broadcasted_iota(I32, (8, LANES), 0)
            strength = jnp.where(rec < counts_ref[0], coef_ref[rows, lanes] * -0.5, 0.0)
            for c in range(comps):
                blade_ref[c, rows, lanes] = strength * (speed_a * a[c] + speed_b * b[c])
    store.wait()


def exchange(groups_x, groups_y, second, *refs):
    if second:
        old, refs = refs[0], refs[1:]
    (field, part_ref, inflow, result, samp_ref,
     y_send, y_recv, x_recv, gathered, mine, send_sem, recv_sem) = refs
    comps, cells_x, cells_y, depth = field.shape
    tile_x, tile_y = lax.axis_index("gx"), lax.axis_index("gy")
    scale = 0.5 if second else 1.0
    last_x = groups_x - 1
    chunk = cells_x // CHUNKS

    def peer(k):
        return lax.rem(tile_y + k, groups_y)

    barrier = pltpu.get_barrier_semaphore()

    @pl.loop(1, groups_y)
    def _(k):
        pl.semaphore_signal(barrier, inc=1, device_id={"gy": peer(k)}, device_id_type=MESH)

    @pl.when(tile_x > 0)
    def _():
        pl.semaphore_signal(barrier, inc=1, device_id={"gx": tile_x - 1}, device_id_type=MESH)

    @pl.when(tile_x < last_x)
    def _():
        pl.semaphore_signal(barrier, inc=1, device_id={"gx": tile_x + 1}, device_id_type=MESH)

    @pl.loop(0, cells_x // 8)
    def _(b):
        rows = pl.ds(b * 8, 8)
        for c in range(comps):
            for half in range(2):
                lanes = pl.ds(half * LANES, LANES)
                y_send[0, half, c, rows, :] = field[c, rows, 0, lanes]
                y_send[1, half, c, rows, :] = field[c, rows, cells_y - 1, lanes]

    @pl.when(tile_x == 0)
    def _():
        x_recv[0] = inflow[...]

    @pl.when(tile_x == last_x)
    def _():
        x_recv[1] = field[:, cells_x - 1]

    neighbours = (tile_x > 0).astype(I32) + (tile_x < last_x).astype(I32)
    pl.semaphore_wait(barrier, groups_y - 1 + neighbours)

    def remote(src, dst, slot, where):
        return pltpu.make_async_remote_copy(
            src_ref=src, dst_ref=dst, send_sem=send_sem.at[slot], recv_sem=recv_sem.at[slot],
            device_id=where, device_id_type=MESH,
        )

    def part_copy(k):
        return remote(part_ref.at[peer(k)], gathered.at[k], k, {"gy": peer(k)})

    def sum_copy(k):
        return remote(mine, samp_ref.at[tile_y], groups_y + k, {"gy": peer(k)})

    def y_copy(q, side):
        rows = pl.ds(q * chunk, chunk)
        return remote(
            y_send.at[1 - side, :, :, rows, :], y_recv.at[side, :, :, rows, :],
            2 * groups_y + 2 * q + side, {"gy": peer(groups_y - 1 if side else 1)},
        )

    x_slot = 2 * groups_y + 2 * CHUNKS
    to_east = remote(field.at[:, cells_x - 1], x_recv.at[0], x_slot, {"gx": tile_x + 1})
    to_west = remote(field.at[:, 0], x_recv.at[1], x_slot + 1, {"gx": tile_x - 1})

    @pl.loop(1, groups_y)
    def _(k):
        part_copy(k).start()

    for q in range(CHUNKS):
        for side in range(2):
            y_copy(q, side).start()

    @pl.when(tile_x < last_x)
    def _():
        to_east.start()

    @pl.when(tile_x > 0)
    def _():
        to_west.start()

    @pl.loop(1, groups_y)
    def _(k):
        part_copy(k).wait_recv()

    total = part_ref[tile_y]
    for k in range(1, groups_y):
        total = total + gathered[k]
    mine[...] = total
    samp_ref[tile_y] = total

    @pl.loop(1, groups_y)
    def _(k):
        sum_copy(k).start()

    row = lax.broadcasted_iota(I32, (cells_y, LANES), 0)
    lane = lax.broadcasted_iota(I32, (cells_y, LANES), 1)
    a = scale * TIME_STEP * VISCOSITY
    b = scale * TIME_STEP * 0.5
    centre = scale * (1.0 - 6.0 * TIME_STEP * VISCOSITY)

    def ghost(side, half, c, i):
        return jnp.concatenate([y_recv[side, half, c, pl.ds(i, 8, stride=0), :]] * (cells_y // 8))

    def plane(i, west, east):
        for half in range(2):
            lanes = pl.ds(half * LANES, LANES)
            others = pl.ds((1 - half) * LANES, LANES)
            bu, bv, bw = (b * field[c, i, :, lanes] for c in range(3))
            for c in range(comps):
                here = field[c, i, :, lanes]
                other = field[c, i, :, others]
                south = jnp.where(row == 0, ghost(0, half, c, i), pltpu.roll(here, 1, 0))
                north = jnp.where(
                    row == cells_y - 1, ghost(1, half, c, i), pltpu.roll(here, cells_y - 1, 0)
                )
                lower = pltpu.roll(here, 1, 1)
                upper = pltpu.roll(here, LANES - 1, 1)
                if half == 0:
                    lower = jnp.where(lane == 0, 0.0, lower)
                    upper = jnp.where(lane == LANES - 1, pltpu.roll(other, LANES - 1, 1), upper)
                else:
                    lower = jnp.where(lane == 0, pltpu.roll(other, 1, 1), lower)
                    upper = jnp.where(lane == LANES - 1, 0.0, upper)
                out = (
                    centre * here
                    + ((a - bu) * east(c, lanes) + (a + bu) * west(c, lanes))
                    + ((a - bv) * north + (a + bv) * south)
                    + ((a - bw) * upper + (a + bw) * lower)
                )
                if second:
                    out = out + 0.5 * old[c, i, :, lanes]
                result[c, i, :, lanes] = out

    for q in range(CHUNKS):
        for side in range(2):
            y_copy(q, side).wait_recv()

        @pl.loop(max(1, q * chunk), min(cells_x - 1, (q + 1) * chunk))
        def _(i):
            plane(
                i,
                lambda c, lanes: field[c, i - 1, :, lanes],
                lambda c, lanes: field[c, i + 1, :, lanes],
            )

    @pl.when(tile_x > 0)
    def _():
        to_east.wait_recv()

    @pl.when(tile_x < last_x)
    def _():
        to_west.wait_recv()

    plane(0, lambda c, lanes: x_recv[0, c, :, lanes], lambda c, lanes: field[c, 1, :, lanes])
    plane(
        cells_x - 1,
        lambda c, lanes: field[c, cells_x - 2, :, lanes],
        lambda c, lanes: x_recv[1, c, :, lanes],
    )

    @pl.loop(1, groups_y)
    def _(k):
        part_copy(k).wait_send()
        sum_copy(k).wait_send()

    for q in range(CHUNKS):
        for side in range(2):
            y_copy(q, side).wait_send()

    @pl.when(tile_x < last_x)
    def _():
        to_east.wait_send()

    @pl.when(tile_x > 0)
    def _():
        to_west.wait_send()

    @pl.loop(1, groups_y)
    def _(k):
        remote(mine, samp_ref.at[peer(groups_y - k)], groups_y + k, {"gy": peer(k)}).wait_recv()


def local(groups_x, groups_y, velocity, inflow, positions, tiles, coefs, counts):
    comps, cells_x, cells_y, depth = velocity.shape
    total_y = cells_y * groups_y
    pos, tiles, coefs = positions[0].transpose(1, 0, 2), tiles[0].T, coefs[0]
    _, recs, points = pos.shape
    velocity = pltpu.with_memory_space_constraint(velocity, pltpu.HBM)
    grid = pltpu.VMEM(velocity.shape, F32)
    table = pltpu.VMEM((groups_y, comps, recs * points // (groups_y * LANES), LANES), F32)
    plan_type = pltpu.SMEM((2, LANES), I32)

    field, part, plan = pl.pallas_call(
        functools.partial(sample_first, total_y, groups_y),
        out_shape=(grid, table, plan_type),
        in_specs=[HBM, VMEM, SMEM, SMEM],
        out_specs=(VMEM, VMEM, SMEM),
        scratch_shapes=[
            pltpu.VMEM((recs, LANES), I32),
            pltpu.SMEM((recs, LANES), I32),
            pltpu.SemaphoreType.DMA((2,)),
        ],
        compiler_params=params(),
        name="sample_first",
    )(velocity, pos, tiles, counts)

    def swap(second, *operands):
        sems = 2 * groups_y + 2 * CHUNKS + 2
        return pl.pallas_call(
            functools.partial(exchange, groups_x, groups_y, second),
            out_shape=(grid, table),
            in_specs=[VMEM] * len(operands),
            out_specs=(VMEM, VMEM),
            scratch_shapes=[
                pltpu.VMEM((2, 2, comps, cells_x, LANES), F32),
                pltpu.VMEM((2, 2, comps, cells_x, LANES), F32),
                pltpu.VMEM((2, comps, cells_y, depth), F32),
                pltpu.VMEM(table.shape, F32),
                pltpu.VMEM(table.shape[1:], F32),
                pltpu.SemaphoreType.DMA((sems,)),
                pltpu.SemaphoreType.DMA((sems,)),
            ],
            compiler_params=params(collective_id=int(second), has_side_effects=True),
            name="exchange_second" if second else "exchange_first",
        )(*operands)

    section, samp_a = swap(False, field, part, inflow)
    section, part = pl.pallas_call(
        functools.partial(spread_and_sample, total_y),
        out_shape=(grid, table),
        in_specs=[SMEM, VMEM, VMEM, VMEM, VMEM],
        out_specs=(VMEM, VMEM),
        input_output_aliases={4: 0},
        compiler_params=params(),
        name="spread_and_sample",
    )(plan, pos, coefs, samp_a, section)
    final, samp_b = swap(True, field, section, part, inflow)
    _, velocity_next, blade = pl.pallas_call(
        functools.partial(spread_last, total_y),
        out_shape=(
            grid,
            jax.ShapeDtypeStruct(velocity.shape, F32),
            jax.ShapeDtypeStruct(pos.shape, F32),
        ),
        in_specs=[SMEM, VMEM, VMEM, SMEM, VMEM, VMEM, VMEM],
        out_specs=(VMEM, HBM, VMEM),
        input_output_aliases={6: 0},
        scratch_shapes=[pltpu.SemaphoreType.DMA((1,))],
        compiler_params=params(),
        name="spread_last",
    )(plan, pos, coefs, counts, samp_a, samp_b, final)
    return (velocity_next, blade.transpose(1, 0, 2)[None])


def solution(mesh):
    return jax.shard_map(
        functools.partial(local, mesh.shape["gx"], mesh.shape["gy"]),
        mesh=mesh,
        in_specs=(
            P(None, "gx", "gy", None),
            P(None, "gy", None),
            P("gx", None, None, None),
            P("gx", None, None),
            P("gx", None, None),
            P("gx"),
        ),
        out_specs=(P(None, "gx", "gy", None), P("gx", None, None, None)),
        check_vma=False,
    )
```

```python
import functools
import math

import jax
import jax.numpy as jnp
from jax import lax
from jax.experimental import pallas as pl
from jax.experimental.pallas import tpu as pltpu
from jax.sharding import PartitionSpec as P

F32, BF16, I32 = jnp.float32, jnp.bfloat16, jnp.int32
RAD = 2
VISCOSITY = 0.05
TIME_STEP = 0.1
WIDTH_EPS = 1.5
K0, K1, K2 = (
    math.exp(-((d / WIDTH_EPS) ** 2)) / (WIDTH_EPS * math.sqrt(math.pi)) for d in range(3)
)
MESH = pl.DeviceIdType.MESH
VMEM = pl.BlockSpec(memory_space=pltpu.VMEM)
SMEM = pl.BlockSpec(memory_space=pltpu.SMEM)
HBM = pl.BlockSpec(memory_space=pltpu.HBM)
LANES = 128
INNER = 4
STEP = 4
PIECES = 4


def params(**kw):
    return pltpu.CompilerParams(vmem_limit_bytes=16 << 20, **kw)


def local_y(pos_y, tile_y, cells_y, total_y):
    return lax.rem(pos_y - tile_y * cells_y + total_y + total_y // 2, total_y) - total_y // 2


def smooth_z(block):
    near = pltpu.roll(block, 1, 1) + pltpu.roll(block, block.shape[1] - 1, 1)
    far = pltpu.roll(block, 2, 1) + pltpu.roll(block, block.shape[1] - 2, 1)
    return K0 * block + K1 * near + K2 * far


def split_dot(block, pick, dims):
    rows = block.shape[0]
    high = block.astype(BF16)
    low = (block - high.astype(F32)).astype(BF16)
    both = lax.dot_general(
        jnp.concatenate([high, low], axis=0), pick, (dims, ((), ())), preferred_element_type=F32
    )
    return both[:rows] + both[rows:]


def point_pick(pos_ref, rec, depth):
    pos_z = pos_ref[2, pl.ds(rec, 1), :]
    cell = lax.broadcasted_iota(I32, (depth, pos_z.shape[1]), 0)
    return (cell == pos_z).astype(F32).astype(BF16)


def weight_y(pos_ref, rec, tile_y, cells_y, total_y):
    here = local_y(pos_ref[1, pl.ds(rec, 1), :], tile_y, cells_y, total_y)
    dist = jnp.abs(lax.broadcasted_iota(I32, (cells_y, here.shape[1]), 0) - here)
    return jnp.where(
        dist == 0, K0, jnp.where(dist == 1, K1, jnp.where(dist == 2, K2, 0.0))
    ).astype(F32)


def sample_record(field, pos_ref, part_ref, rec, hub, tile_y, total_y):
    comps, _, cells_y, depth = field.shape
    planes = (
        K0 * field[:, hub]
        + K1 * (field[:, hub - 1] + field[:, hub + 1])
        + K2 * (field[:, hub - 2] + field[:, hub + 2])
    )
    smooth = smooth_z(planes.reshape(comps * cells_y, depth))
    inner = split_dot(smooth, point_pick(pos_ref, rec, depth), ((1,), (0,)))
    along = weight_y(pos_ref, rec, tile_y, cells_y, total_y)
    value = jnp.sum(inner.reshape(comps, cells_y, -1) * along[None], axis=1)
    group, row = rec // 8, lax.rem(rec, 8)
    for half in range(2):
        for c in range(comps):
            part_ref[half * 8 + group, c, pl.ds(row, 1), :] = value[
                c : c + 1, half * LANES : (half + 1) * LANES
            ]


def spread_record(field, pos_ref, coef_ref, samp_ref, rec, hub, scale, tile_y, total_y):
    comps, _, cells_y, depth = field.shape
    group, row = rec // 8, lax.rem(rec, 8)
    sampled = [
        jnp.concatenate(
            [samp_ref[half * 8 + group, c, pl.ds(row, 1), :] for half in range(2)], axis=1
        )
        for c in range(comps)
    ]
    speed = jnp.sqrt(sampled[0] * sampled[0] + sampled[1] * sampled[1] + sampled[2] * sampled[2])
    strength = coef_ref[pl.ds(rec, 1), :] * speed * (-scale)
    along = weight_y(pos_ref, rec, tile_y, cells_y, total_y)
    weighted = jnp.concatenate([along * (strength * value) for value in sampled], axis=0)
    slab = split_dot(weighted, point_pick(pos_ref, rec, depth), ((1,), (1,)))
    slab = smooth_z(slab).reshape(comps, cells_y, depth)
    for d, weight in ((-2, K2), (-1, K1), (0, K0), (1, K1), (2, K2)):
        field[:, hub + d] += weight * slab


def sample_first(total_y, groups_y, vel_hbm, pos_ref, tiles_ref, counts_ref,
                 field, part_ref, plan_ref, flags, table, sems):
    recs = pos_ref.shape[1]
    cells_x, cells_y = field.shape[1:3]
    tile_x, tile_y = lax.axis_index("gx"), lax.axis_index("gy")
    load = pltpu.make_async_copy(vel_hbm, field, sems.at[0])
    load.start()
    part_ref[...] = jnp.zeros_like(part_ref)
    here = local_y(pos_ref[1], tile_y, cells_y, total_y)
    near = ((here >= -RAD) & (here < cells_y + RAD)).astype(I32)
    touched = jnp.max(near, axis=1, keepdims=True)
    hub = pos_ref[0, :, 0:LANES] - tile_x * cells_x
    flags[...] = jnp.where(touched > 0, hub, -1)
    fetch = pltpu.make_async_copy(flags, table, sems.at[1])
    fetch.start()
    fetch.wait()

    def place(rec, count):
        hub = table[rec, 0]
        listed = lax.rem(tile_y - tiles_ref[0, rec] + groups_y, groups_y) < tiles_ref[1, rec]
        plan_ref[0, count] = rec
        plan_ref[1, count] = hub
        take = listed & (rec < counts_ref[0]) & (hub >= 0)
        return count + take.astype(I32)

    count = lax.fori_loop(0, recs, place, jnp.int32(0))
    plan_ref[0, LANES - 1] = count
    load.wait()

    @pl.loop(0, count)
    def _(n):
        sample_record(field, pos_ref, part_ref, plan_ref[0, n], plan_ref[1, n], tile_y, total_y)


def spread_and_sample(total_y, plan_ref, pos_ref, coef_ref, samp_ref, _, field, part_ref):
    tile_y = lax.axis_index("gy")
    count = plan_ref[0, LANES - 1]
    part_ref[...] = jnp.zeros_like(part_ref)

    @pl.loop(0, count)
    def _(n):
        spread_record(field, pos_ref, coef_ref, samp_ref, plan_ref[0, n], plan_ref[1, n],
                      TIME_STEP, tile_y, total_y)

    @pl.loop(0, count)
    def _(n):
        sample_record(field, pos_ref, part_ref, plan_ref[0, n], plan_ref[1, n], tile_y, total_y)


def spread_last(total_y, plan_ref, pos_ref, coef_ref, counts_ref, samp_a, samp_b, _,
                field, next_hbm, blade_ref, sems):
    tile_y = lax.axis_index("gy")
    comps, recs, _ = blade_ref.shape
    count = plan_ref[0, LANES - 1]

    @pl.loop(0, count)
    def _(n):
        spread_record(field, pos_ref, coef_ref, samp_b, plan_ref[0, n], plan_ref[1, n],
                      0.5 * TIME_STEP, tile_y, total_y)

    store = pltpu.make_async_copy(field, next_hbm, sems.at[0])
    store.start()
    for half in range(2):
        lanes = pl.ds(half * LANES, LANES)
        for group in range(recs // 8):
            rows = pl.ds(group * 8, 8)
            a = [samp_a[half * 8 + group, c] for c in range(comps)]
            b = [samp_b[half * 8 + group, c] for c in range(comps)]
            speed_a = jnp.sqrt(a[0] * a[0] + a[1] * a[1] + a[2] * a[2])
            speed_b = jnp.sqrt(b[0] * b[0] + b[1] * b[1] + b[2] * b[2])
            rec = group * 8 + lax.broadcasted_iota(I32, (8, LANES), 0)
            strength = jnp.where(rec < counts_ref[0], coef_ref[rows, lanes] * -0.5, 0.0)
            for c in range(comps):
                blade_ref[c, rows, lanes] = strength * (speed_a * a[c] + speed_b * b[c])
    store.wait()


def exchange(groups_x, groups_y, second, *refs):
    if second:
        old, refs = refs[0], refs[1:]
    (field, part_ref, inflow, result, samp_ref, y_send, y_recv, x_recv,
     outer_parts, outer_sums, inner_parts, mine, send_sem, recv_sem) = refs
    comps, cells_x, cells_y, depth = field.shape
    tile_x, tile_y = lax.axis_index("gx"), lax.axis_index("gy")
    last_x = groups_x - 1
    outer = groups_y // INNER
    at_outer, at_inner = tile_y // INNER, lax.rem(tile_y, INNER)
    north, south = lax.rem(tile_y + 1, groups_y), lax.rem(tile_y + groups_y - 1, groups_y)

    def outer_tile(k):
        return lax.rem(at_outer + k, outer)

    def inner_tile(k):
        return lax.rem(at_inner + k, INNER)

    barrier = pltpu.get_barrier_semaphore()
    greeted = [outer_tile(k) * INNER + at_inner for k in range(1, outer)]
    greeted += [at_outer * INNER + inner_tile(k) for k in range(1, INNER)]
    greeted += [north, south]
    for where in greeted:
        pl.semaphore_signal(barrier, inc=1, device_id={"gy": where}, device_id_type=MESH)

    @pl.when(tile_x > 0)
    def _():
        pl.semaphore_signal(barrier, inc=1, device_id={"gx": tile_x - 1}, device_id_type=MESH)

    @pl.when(tile_x < last_x)
    def _():
        pl.semaphore_signal(barrier, inc=1, device_id={"gx": tile_x + 1}, device_id_type=MESH)

    @pl.loop(0, cells_x // 8)
    def _(block):
        rows = pl.ds(block * 8, 8)
        for c in range(comps):
            for half in range(2):
                lanes = pl.ds(half * LANES, LANES)
                y_send[0, half, c, rows, :] = field[c, rows, 0, lanes]
                y_send[1, half, c, rows, :] = field[c, rows, cells_y - 1, lanes]

    @pl.when(tile_x == 0)
    def _():
        x_recv[0] = inflow[...]

    @pl.when(tile_x == last_x)
    def _():
        x_recv[1] = field[:, cells_x - 1]

    neighbours = (tile_x > 0).astype(I32) + (tile_x < last_x).astype(I32)
    pl.semaphore_wait(barrier, len(greeted) + neighbours)

    def remote(src, dst, slot, where):
        return pltpu.make_async_remote_copy(
            src_ref=src, dst_ref=dst, send_sem=send_sem.at[slot], recv_sem=recv_sem.at[slot],
            device_id=where, device_id_type=MESH,
        )

    def scatter_outer(k):
        there = outer_tile(k)
        return remote(part_ref.at[pl.ds(there * INNER, INNER)], outer_parts.at[k - 1], k - 1,
                      {"gy": there * INNER + at_inner})

    def scatter_inner(k):
        there = inner_tile(k)
        return remote(outer_sums.at[there], inner_parts.at[k - 1], outer + k - 2,
                      {"gy": at_outer * INNER + there})

    base = outer + INNER - 2

    def gather_inner(k, from_tile):
        return remote(mine, samp_ref.at[from_tile], base + k - 1,
                      {"gy": at_outer * INNER + inner_tile(k)})

    def gather_outer(k, from_outer):
        block = pl.ds(from_outer * INNER, INNER)
        return remote(samp_ref.at[pl.ds(at_outer * INNER, INNER)], samp_ref.at[block],
                      base + INNER + k - 2, {"gy": outer_tile(k) * INNER + at_inner})

    to_north = remote(y_send.at[1], y_recv.at[0], 2 * base, {"gy": north})
    to_south = remote(y_send.at[0], y_recv.at[1], 2 * base + 1, {"gy": south})
    to_east = remote(field.at[:, cells_x - 1], x_recv.at[0], 2 * base + 2, {"gx": tile_x + 1})
    to_west = remote(field.at[:, 0], x_recv.at[1], 2 * base + 3, {"gx": tile_x - 1})

    for k in range(1, outer):
        scatter_outer(k).start()
    to_north.start()
    to_south.start()

    @pl.when(tile_x < last_x)
    def _():
        to_east.start()

    @pl.when(tile_x > 0)
    def _():
        to_west.start()

    scale = 0.5 if second else 1.0
    a = scale * TIME_STEP * VISCOSITY
    b = scale * TIME_STEP * 0.5
    centre = scale * (1.0 - 6.0 * TIME_STEP * VISCOSITY)
    sub = lax.broadcasted_iota(I32, (8, LANES), 0)
    lane = lax.broadcasted_iota(I32, (8, LANES), 1)
    first_row, last_row = sub == 0, sub == 7
    first_lane, last_lane = lane == 0, lane == LANES - 1
    zero = jnp.zeros((8, LANES), F32)
    halves = [pl.ds(half * LANES, LANES) for half in range(2)]
    strips = cells_y // 8

    def tile(c, i, t, half):
        return field[c, i, pl.ds(8 * t, 8), halves[half]]

    def ghost(side, half, c, i):
        return y_recv[side, half, c, pl.ds(i, 8, stride=0), :]

    def plane(i, west, east, ghosts):
        for t in range(strips):
            rows = pl.ds(8 * t, 8)
            here = [[tile(c, i, t, half) for half in range(2)] for c in range(comps)]
            lower, upper = [], []
            for c in range(comps):
                up = [pltpu.roll(v, 1, 1) for v in here[c]]
                down = [pltpu.roll(v, LANES - 1, 1) for v in here[c]]
                lower.append([jnp.where(first_lane, zero, up[0]), jnp.where(first_lane, up[0], up[1])])
                upper.append([jnp.where(last_lane, down[1], down[0]), jnp.where(last_lane, zero, down[1])])
            for half in range(2):
                bu, bv, bw = (b * here[c][half] for c in range(3))
                for c in range(comps):
                    if t > 0:
                        below = pltpu.roll(tile(c, i, t - 1, half), 1, 0)
                    else:
                        below = ghost(0, half, c, i) if ghosts else zero
                    if t < strips - 1:
                        above = pltpu.roll(tile(c, i, t + 1, half), 7, 0)
                    else:
                        above = ghost(1, half, c, i) if ghosts else zero
                    value = here[c][half]
                    to_s = jnp.where(first_row, below, pltpu.roll(value, 1, 0))
                    to_n = jnp.where(last_row, above, pltpu.roll(value, 7, 0))
                    out = (
                        centre * value
                        + ((a - bu) * east(c, rows, halves[half]) + (a + bu) * west(c, rows, halves[half]))
                        + ((a - bv) * to_n + (a + bv) * to_s)
                        + ((a - bw) * upper[c][half] + (a + bw) * lower[c][half])
                    )
                    if second:
                        out = out + 0.5 * old[c, i, rows, halves[half]]
                    result[c, i, rows, halves[half]] = out

    def inside(i, ghosts):
        plane(
            i,
            lambda c, rows, lanes: field[c, i - 1, rows, lanes],
            lambda c, rows, lanes: field[c, i + 1, rows, lanes],
            ghosts,
        )

    def piece(start, stop, ghosts):
        @pl.loop(0, (stop - start) // STEP)
        def _(n):
            for k in range(STEP):
                inside(start + n * STEP + k, ghosts)

    steps = (cells_x - 2) // STEP
    cuts = [1 + STEP * (steps * k // PIECES) for k in range(PIECES + 1)]

    piece(cuts[0], cuts[1], False)
    for k in range(1, outer):
        scatter_outer(k).wait_recv()
    outer_sums[...] = functools.reduce(
        jnp.add, [outer_parts[k] for k in range(outer - 1)], part_ref[pl.ds(at_outer * INNER, INNER)]
    )
    for k in range(1, INNER):
        scatter_inner(k).start()
    piece(cuts[1], cuts[2], False)
    for k in range(1, INNER):
        scatter_inner(k).wait_recv()
    total = functools.reduce(jnp.add, [inner_parts[k] for k in range(INNER - 1)], outer_sums[at_inner])
    mine[...] = total
    samp_ref[tile_y] = total
    for k in range(1, INNER):
        gather_inner(k, tile_y).start()
    piece(cuts[2], cuts[3], False)
    for k in range(1, INNER):
        gather_inner(k, at_outer * INNER + inner_tile(INNER - k)).wait_recv()
    for k in range(1, outer):
        gather_outer(k, at_outer).start()
    to_north.wait_recv()
    to_south.wait_recv()
    piece(cuts[3], cuts[4], True)
    for i in range(cuts[4], cells_x - 1):
        inside(i, True)

    @pl.when(tile_x > 0)
    def _():
        to_east.wait_recv()

    @pl.when(tile_x < last_x)
    def _():
        to_west.wait_recv()

    plane(
        0,
        lambda c, rows, lanes: x_recv[0, c, rows, lanes],
        lambda c, rows, lanes: field[c, 1, rows, lanes],
        True,
    )
    plane(
        cells_x - 1,
        lambda c, rows, lanes: field[c, cells_x - 2, rows, lanes],
        lambda c, rows, lanes: x_recv[1, c, rows, lanes],
        True,
    )

    @pl.loop(0, (cuts[3] - cuts[0]) // STEP)
    def _(n):
        for k in range(STEP):
            i = cuts[0] + n * STEP + k
            for side, t, mask in ((0, 0, first_row), (1, strips - 1, last_row)):
                rows = pl.ds(8 * t, 8)
                for half in range(2):
                    bv = b * tile(1, i, t, half)
                    weight = jnp.where(mask, a - bv if side else a + bv, 0.0)
                    for c in range(comps):
                        before = result[c, i, rows, halves[half]]
                        result[c, i, rows, halves[half]] = before + weight * ghost(side, half, c, i)

    for k in range(1, outer):
        gather_outer(k, outer_tile(outer - k)).wait_recv()
    for k in range(1, outer):
        scatter_outer(k).wait_send()
        gather_outer(k, at_outer).wait_send()
    for k in range(1, INNER):
        scatter_inner(k).wait_send()
        gather_inner(k, tile_y).wait_send()
    to_north.wait_send()
    to_south.wait_send()

    @pl.when(tile_x < last_x)
    def _():
        to_east.wait_send()

    @pl.when(tile_x > 0)
    def _():
        to_west.wait_send()


def local(groups_x, groups_y, velocity, inflow, positions, tiles, coefs, counts):
    comps, cells_x, cells_y, depth = velocity.shape
    total_y = cells_y * groups_y
    pos, tiles, coefs = positions[0].transpose(1, 0, 2), tiles[0].T, coefs[0]
    _, recs, points = pos.shape
    velocity = pltpu.with_memory_space_constraint(velocity, pltpu.HBM)
    grid = pltpu.VMEM(velocity.shape, F32)
    table = pltpu.VMEM((groups_y, comps, recs * points // (groups_y * LANES), LANES), F32)
    plan_type = pltpu.SMEM((2, LANES), I32)

    field, part, plan = pl.pallas_call(
        functools.partial(sample_first, total_y, groups_y),
        out_shape=(grid, table, plan_type),
        in_specs=[HBM, VMEM, SMEM, SMEM],
        out_specs=(VMEM, VMEM, SMEM),
        scratch_shapes=[
            pltpu.VMEM((recs, LANES), I32),
            pltpu.SMEM((recs, LANES), I32),
            pltpu.SemaphoreType.DMA((2,)),
        ],
        compiler_params=params(),
        name="sample_first",
    )(velocity, pos, tiles, counts)

    def swap(second, *operands):
        outer = groups_y // INNER
        sems = 2 * (outer + INNER - 2) + 4
        return pl.pallas_call(
            functools.partial(exchange, groups_x, groups_y, second),
            out_shape=(grid, table),
            in_specs=[VMEM] * len(operands),
            out_specs=(VMEM, VMEM),
            scratch_shapes=[
                pltpu.VMEM((2, 2, comps, cells_x, LANES), F32),
                pltpu.VMEM((2, 2, comps, cells_x, LANES), F32),
                pltpu.VMEM((2, comps, cells_y, depth), F32),
                pltpu.VMEM((outer - 1, INNER, *table.shape[1:]), F32),
                pltpu.VMEM((INNER, *table.shape[1:]), F32),
                pltpu.VMEM((INNER - 1, *table.shape[1:]), F32),
                pltpu.VMEM(table.shape[1:], F32),
                pltpu.SemaphoreType.DMA((sems,)),
                pltpu.SemaphoreType.DMA((sems,)),
            ],
            compiler_params=params(collective_id=int(second), has_side_effects=True),
            name="exchange_second" if second else "exchange_first",
        )(*operands)

    section, samp_a = swap(False, field, part, inflow)
    section, part = pl.pallas_call(
        functools.partial(spread_and_sample, total_y),
        out_shape=(grid, table),
        in_specs=[SMEM, VMEM, VMEM, VMEM, VMEM],
        out_specs=(VMEM, VMEM),
        input_output_aliases={4: 0},
        compiler_params=params(),
        name="spread_and_sample",
    )(plan, pos, coefs, samp_a, section)
    final, samp_b = swap(True, field, section, part, inflow)
    _, velocity_next, blade = pl.pallas_call(
        functools.partial(spread_last, total_y),
        out_shape=(
            grid,
            jax.ShapeDtypeStruct(velocity.shape, F32),
            jax.ShapeDtypeStruct(pos.shape, F32),
        ),
        in_specs=[SMEM, VMEM, VMEM, SMEM, VMEM, VMEM, VMEM],
        out_specs=(VMEM, HBM, VMEM),
        input_output_aliases={6: 0},
        scratch_shapes=[pltpu.SemaphoreType.DMA((1,))],
        compiler_params=params(),
        name="spread_last",
    )(plan, pos, coefs, counts, samp_a, samp_b, final)
    return (velocity_next, blade.transpose(1, 0, 2)[None])


def solution(mesh):
    return jax.shard_map(
        functools.partial(local, mesh.shape["gx"], mesh.shape["gy"]),
        mesh=mesh,
        in_specs=(
            P(None, "gx", "gy", None),
            P(None, "gy", None),
            P("gx", None, None, None),
            P("gx", None, None),
            P("gx", None, None),
            P("gx"),
        ),
        out_specs=(P(None, "gx", "gy", None), P("gx", None, None, None)),
        check_vma=False,
    )
```

```python
import functools
import math

import jax
import jax.numpy as jnp
from jax import lax
from jax.experimental import pallas as pl
from jax.experimental.pallas import tpu as pltpu
from jax.sharding import PartitionSpec as P

F32, BF16, I32 = jnp.float32, jnp.bfloat16, jnp.int32
RAD = 2
VISCOSITY = 0.05
TIME_STEP = 0.1
WIDTH_EPS = 1.5
K0, K1, K2 = (
    math.exp(-((d / WIDTH_EPS) ** 2)) / (WIDTH_EPS * math.sqrt(math.pi)) for d in range(3)
)
MESH = pl.DeviceIdType.MESH
VMEM = pl.BlockSpec(memory_space=pltpu.VMEM)
SMEM = pl.BlockSpec(memory_space=pltpu.SMEM)
HBM = pl.BlockSpec(memory_space=pltpu.HBM)
LANES = 128
STEP = 4
CHUNKS = 4


def params(**kw):
    return pltpu.CompilerParams(vmem_limit_bytes=16 << 20, **kw)


def local_y(pos_y, tile_y, cells_y, total_y):
    return lax.rem(pos_y - tile_y * cells_y + total_y + total_y // 2, total_y) - total_y // 2


def smooth_z(block):
    near = pltpu.roll(block, 1, 1) + pltpu.roll(block, block.shape[1] - 1, 1)
    far = pltpu.roll(block, 2, 1) + pltpu.roll(block, block.shape[1] - 2, 1)
    return K0 * block + K1 * near + K2 * far


def split_dot(block, pick, dims):
    rows = block.shape[0]
    high = block.astype(BF16)
    low = (block - high.astype(F32)).astype(BF16)
    both = lax.dot_general(
        jnp.concatenate([high, low], axis=0), pick, (dims, ((), ())), preferred_element_type=F32
    )
    return both[:rows] + both[rows:]


def build_tables(pos_ref, pick_ref, along_ref, n, rec, tile_y, total_y):
    depth, points = pick_ref.shape[1:]
    cells_y = along_ref.shape[1]
    cell = lax.broadcasted_iota(I32, (depth, points), 0)
    pick_ref[n] = (cell == pos_ref[2, pl.ds(rec, 1), :]).astype(F32).astype(BF16)
    here = local_y(pos_ref[1, pl.ds(rec, 1), :], tile_y, cells_y, total_y)
    dist = jnp.abs(lax.broadcasted_iota(I32, (cells_y, points), 0) - here)
    along_ref[n] = jnp.where(
        dist == 0, K0, jnp.where(dist == 1, K1, jnp.where(dist == 2, K2, 0.0))
    ).astype(F32)


def sample_pair(field, plan_ref, pick_ref, along_ref, part_ref, pair, count):
    comps, _, cells_y, depth = field.shape
    for n in (2 * pair, jnp.minimum(2 * pair + 1, count - 1)):
        rec, hub = plan_ref[0, n], plan_ref[1, n]
        planes = (
            K0 * field[:, hub]
            + K1 * (field[:, hub - 1] + field[:, hub + 1])
            + K2 * (field[:, hub - 2] + field[:, hub + 2])
        )
        smooth = smooth_z(planes.reshape(comps * cells_y, depth))
        inner = split_dot(smooth, pick_ref[n], ((1,), (0,)))
        value = jnp.sum(inner.reshape(comps, cells_y, -1) * along_ref[n][None], axis=1)
        group, row = rec // 8, lax.rem(rec, 8)
        for half in range(2):
            for c in range(comps):
                part_ref[half * 8 + group, c, pl.ds(row, 1), :] = value[
                    c : c + 1, half * LANES : (half + 1) * LANES
                ]


def spread_pair(field, plan_ref, pick_ref, along_ref, coef_ref, samp_ref, scale, pair, count):
    comps, _, cells_y, depth = field.shape
    slabs = []
    for k in range(2):
        n = jnp.minimum(2 * pair + k, count - 1)
        rec, hub = plan_ref[0, n], plan_ref[1, n]
        factor = jnp.where(2 * pair + k < count, -scale, 0.0)
        group, row = rec // 8, lax.rem(rec, 8)
        sampled = [
            jnp.concatenate(
                [samp_ref[half * 8 + group, c, pl.ds(row, 1), :] for half in range(2)], axis=1
            )
            for c in range(comps)
        ]
        speed = jnp.sqrt(sampled[0] * sampled[0] + sampled[1] * sampled[1] + sampled[2] * sampled[2])
        strength = coef_ref[pl.ds(rec, 1), :] * speed * factor
        along = along_ref[n]
        weighted = jnp.concatenate([along * (strength * value) for value in sampled], axis=0)
        slab = smooth_z(split_dot(weighted, pick_ref[n], ((1,), (1,))))
        slabs.append((hub, slab.reshape(comps, cells_y, depth)))
    for hub, slab in slabs:
        for d, weight in ((-2, K2), (-1, K1), (0, K0), (1, K1), (2, K2)):
            field[:, hub + d] += weight * slab


def make_plan(total_y, groups_y, pos_ref, tiles_ref, counts_ref, rows_ref, cells_x, cells_y):
    recs = pos_ref.shape[1]
    tile_x, tile_y = lax.axis_index("gx"), lax.axis_index("gy")
    rec = lax.broadcasted_iota(I32, (recs, LANES), 0)
    lane = lax.broadcasted_iota(I32, (recs, LANES), 1)
    square = lax.broadcasted_iota(I32, (recs, recs), 0) == lax.broadcasted_iota(I32, (recs, recs), 1)

    def column(row):
        return jnp.sum(jnp.where(square, row.astype(F32), 0.0), axis=1, keepdims=True).astype(I32)

    here = local_y(pos_ref[1], tile_y, cells_y, total_y)
    near = ((here >= -RAD) & (here < cells_y + RAD)).astype(I32)
    touched = jnp.max(near, axis=1, keepdims=True)
    hub = pos_ref[0, :, 0:1] - tile_x * cells_x
    first, number = column(tiles_ref[0:1, :]), column(tiles_ref[1:2, :])
    listed = lax.rem(tile_y - first + groups_y, groups_y) < number
    active = listed & (touched > 0) & (rec[:, 0:1] < counts_ref[0])
    big = jnp.int32(1 << 20)
    key = jnp.where(active, hub * recs + rec[:, 0:1], big)
    key_row = jnp.min(jnp.where(rec == lane, key, big), axis=0, keepdims=True)
    rank = jnp.sum((key_row < key).astype(F32), axis=1, keepdims=True).astype(I32)
    live = active.astype(F32)
    count = jnp.sum(live, axis=0, keepdims=True).astype(I32)
    mine = active & (rank == jnp.minimum(lane, count - 1))
    rows_ref[0:1, :] = jnp.sum(jnp.where(mine, rec, 0).astype(F32), axis=0, keepdims=True).astype(I32)
    rows_ref[1:2, :] = jnp.sum(jnp.where(mine, hub, 0).astype(F32), axis=0, keepdims=True).astype(I32)
    below = active & (hub < lane)
    rows_ref[2:3, :] = jnp.sum(below.astype(F32), axis=0, keepdims=True).astype(I32)


def sample_first(total_y, groups_y, vel_hbm, pos_hbm, tiles_hbm, counts_ref,
                 field, pos_ref, part_ref, plan_ref, pick_ref, along_ref, tiles_ref, rows_ref, sems):
    cells_x, cells_y = field.shape[1:3]
    tile_y = lax.axis_index("gy")
    chunk = cells_x // CHUNKS
    fetch_pos = pltpu.make_async_copy(pos_hbm, pos_ref, sems.at[CHUNKS])
    fetch_tiles = pltpu.make_async_copy(tiles_hbm, tiles_ref, sems.at[CHUNKS + 1])
    fetch_pos.start()
    fetch_tiles.start()
    loads = []
    for q in range(CHUNKS):
        planes = pl.ds(q * chunk, chunk)
        loads.append(pltpu.make_async_copy(vel_hbm.at[:, planes], field.at[:, planes], sems.at[q]))
        loads[-1].start()
    part_ref[...] = jnp.zeros_like(part_ref)
    rows_ref[...] = jnp.zeros_like(rows_ref)
    fetch_pos.wait()
    fetch_tiles.wait()
    make_plan(total_y, groups_y, pos_ref, tiles_ref, counts_ref, rows_ref, cells_x, cells_y)
    fetch_plan = pltpu.make_async_copy(rows_ref, plan_ref, sems.at[CHUNKS + 2])
    fetch_plan.start()
    fetch_plan.wait()
    count = plan_ref[2, LANES - 1]

    @pl.loop(0, count)
    def _(n):
        build_tables(pos_ref, pick_ref, along_ref, n, plan_ref[0, n], tile_y, total_y)

    start = jnp.int32(0)
    for q in range(CHUNKS):
        loads[q].wait()
        if q < CHUNKS - 1:
            stop = plan_ref[2, (q + 1) * chunk - RAD] // 2
        else:
            stop = (count + 1) // 2

        @pl.loop(start, stop)
        def _(pair):
            sample_pair(field, plan_ref, pick_ref, along_ref, part_ref, pair, count)

        start = stop


def spread_and_sample(plan_ref, pick_ref, along_ref, coef_ref, samp_ref, _, field, part_ref):
    count = plan_ref[2, LANES - 1]
    part_ref[...] = jnp.zeros_like(part_ref)

    @pl.loop(0, (count + 1) // 2)
    def _(pair):
        spread_pair(field, plan_ref, pick_ref, along_ref, coef_ref, samp_ref, TIME_STEP, pair, count)

    @pl.loop(0, (count + 1) // 2)
    def _(pair):
        sample_pair(field, plan_ref, pick_ref, along_ref, part_ref, pair, count)


def spread_last(plan_ref, pick_ref, along_ref, coef_ref, counts_ref, samp_a, samp_b, _,
                field, next_hbm, blade_ref, sems):
    comps, recs, _ = blade_ref.shape
    chunk = field.shape[1] // CHUNKS
    count = plan_ref[2, LANES - 1]
    start = jnp.int32(0)
    stores = []
    for q in range(CHUNKS):
        if q < CHUNKS - 1:
            stop = (plan_ref[2, (q + 1) * chunk + RAD] + 1) // 2
        else:
            stop = (count + 1) // 2

        @pl.loop(start, stop)
        def _(pair):
            spread_pair(field, plan_ref, pick_ref, along_ref, coef_ref, samp_b,
                        0.5 * TIME_STEP, pair, count)

        planes = pl.ds(q * chunk, chunk)
        stores.append(pltpu.make_async_copy(field.at[:, planes], next_hbm.at[:, planes], sems.at[q]))
        stores[-1].start()
        start = stop

    for half in range(2):
        lanes = pl.ds(half * LANES, LANES)
        for group in range(recs // 8):
            rows = pl.ds(group * 8, 8)
            a = [samp_a[half * 8 + group, c] for c in range(comps)]
            b = [samp_b[half * 8 + group, c] for c in range(comps)]
            speed_a = jnp.sqrt(a[0] * a[0] + a[1] * a[1] + a[2] * a[2])
            speed_b = jnp.sqrt(b[0] * b[0] + b[1] * b[1] + b[2] * b[2])
            rec = group * 8 + lax.broadcasted_iota(I32, (8, LANES), 0)
            strength = jnp.where(rec < counts_ref[0], coef_ref[rows, lanes] * -0.5, 0.0)
            for c in range(comps):
                blade_ref[c, rows, lanes] = strength * (speed_a * a[c] + speed_b * b[c])
    for store in stores:
        store.wait()


def exchange(groups_x, groups_y, second, *refs):
    if second:
        old, refs = refs[0], refs[1:]
    (field, part_ref, inflow, result, samp_ref,
     y_send, y_recv, x_recv, gathered, mine, send_sem, recv_sem) = refs
    comps, cells_x, cells_y, depth = field.shape
    tile_x, tile_y = lax.axis_index("gx"), lax.axis_index("gy")
    last_x = groups_x - 1

    def peer(k):
        return lax.rem(tile_y + k, groups_y)

    north, south = peer(1), peer(groups_y - 1)
    barrier = pltpu.get_barrier_semaphore()
    for k in range(1, groups_y):
        pl.semaphore_signal(barrier, inc=1, device_id={"gy": peer(k)}, device_id_type=MESH)

    @pl.when(tile_x > 0)
    def _():
        pl.semaphore_signal(barrier, inc=1, device_id={"gx": tile_x - 1}, device_id_type=MESH)

    @pl.when(tile_x < last_x)
    def _():
        pl.semaphore_signal(barrier, inc=1, device_id={"gx": tile_x + 1}, device_id_type=MESH)

    @pl.loop(0, cells_x // 8)
    def _(block):
        rows = pl.ds(block * 8, 8)
        for c in range(comps):
            for half in range(2):
                lanes = pl.ds(half * LANES, LANES)
                y_send[0, half, c, rows, :] = field[c, rows, 0, lanes]
                y_send[1, half, c, rows, :] = field[c, rows, cells_y - 1, lanes]

    @pl.when(tile_x == 0)
    def _():
        x_recv[0] = inflow[...]

    @pl.when(tile_x == last_x)
    def _():
        x_recv[1] = field[:, cells_x - 1]

    neighbours = (tile_x > 0).astype(I32) + (tile_x < last_x).astype(I32)
    pl.semaphore_wait(barrier, groups_y - 1 + neighbours)

    def remote(src, dst, slot, where):
        return pltpu.make_async_remote_copy(
            src_ref=src, dst_ref=dst, send_sem=send_sem.at[slot], recv_sem=recv_sem.at[slot],
            device_id=where, device_id_type=MESH,
        )

    def part_copy(k):
        return remote(part_ref.at[peer(k)], gathered.at[k - 1], k - 1, {"gy": peer(k)})

    def sum_copy(k, owner):
        return remote(mine, samp_ref.at[owner], groups_y + k - 2, {"gy": peer(k)})

    base = groups_y - 1
    to_north = remote(y_send.at[1], y_recv.at[0], 2 * base, {"gy": north})
    to_south = remote(y_send.at[0], y_recv.at[1], 2 * base + 1, {"gy": south})
    to_east = remote(field.at[:, cells_x - 1], x_recv.at[0], 2 * base + 2, {"gx": tile_x + 1})
    to_west = remote(field.at[:, 0], x_recv.at[1], 2 * base + 3, {"gx": tile_x - 1})

    for k in range(1, groups_y):
        part_copy(k).start()
    to_north.start()
    to_south.start()

    @pl.when(tile_x < last_x)
    def _():
        to_east.start()

    @pl.when(tile_x > 0)
    def _():
        to_west.start()

    scale = 0.5 if second else 1.0
    a = scale * TIME_STEP * VISCOSITY
    b = scale * TIME_STEP * 0.5
    centre = scale * (1.0 - 6.0 * TIME_STEP * VISCOSITY)
    sub = lax.broadcasted_iota(I32, (8, LANES), 0)
    lane = lax.broadcasted_iota(I32, (8, LANES), 1)
    first_row, last_row = sub == 0, sub == 7
    first_lane, last_lane = lane == 0, lane == LANES - 1
    zero = jnp.zeros((8, LANES), F32)
    halves = [pl.ds(half * LANES, LANES) for half in range(2)]
    strips = cells_y // 8

    def tile(c, i, t, half):
        return field[c, i, pl.ds(8 * t, 8), halves[half]]

    def ghost(side, half, c, i):
        return y_recv[side, half, c, pl.ds(i, 8, stride=0), :]

    def plane(i, west, east, ghosts):
        for t in range(strips):
            rows = pl.ds(8 * t, 8)
            here = [[tile(c, i, t, half) for half in range(2)] for c in range(comps)]
            lower, upper = [], []
            for c in range(comps):
                up = [pltpu.roll(v, 1, 1) for v in here[c]]
                down = [pltpu.roll(v, LANES - 1, 1) for v in here[c]]
                lower.append([jnp.where(first_lane, zero, up[0]), jnp.where(first_lane, up[0], up[1])])
                upper.append([jnp.where(last_lane, down[1], down[0]), jnp.where(last_lane, zero, down[1])])
            for half in range(2):
                bu, bv, bw = (b * here[c][half] for c in range(3))
                for c in range(comps):
                    if t > 0:
                        below = pltpu.roll(tile(c, i, t - 1, half), 1, 0)
                    else:
                        below = ghost(0, half, c, i) if ghosts else zero
                    if t < strips - 1:
                        above = pltpu.roll(tile(c, i, t + 1, half), 7, 0)
                    else:
                        above = ghost(1, half, c, i) if ghosts else zero
                    value = here[c][half]
                    to_s = jnp.where(first_row, below, pltpu.roll(value, 1, 0))
                    to_n = jnp.where(last_row, above, pltpu.roll(value, 7, 0))
                    out = (
                        centre * value
                        + ((a - bu) * east(c, rows, halves[half]) + (a + bu) * west(c, rows, halves[half]))
                        + ((a - bv) * to_n + (a + bv) * to_s)
                        + ((a - bw) * upper[c][half] + (a + bw) * lower[c][half])
                    )
                    if second:
                        out = out + 0.5 * old[c, i, rows, halves[half]]
                    result[c, i, rows, halves[half]] = out

    def inside(i, ghosts):
        plane(
            i,
            lambda c, rows, lanes: field[c, i - 1, rows, lanes],
            lambda c, rows, lanes: field[c, i + 1, rows, lanes],
            ghosts,
        )

    def piece(start, stop, ghosts):
        @pl.loop(0, (stop - start) // STEP)
        def _(n):
            for k in range(STEP):
                inside(start + n * STEP + k, ghosts)

    steps = (cells_x - 2) // STEP
    cuts = [1 + STEP * (steps * k // 4) for k in (0, 2, 3, 4)]

    piece(cuts[0], cuts[1], False)
    for k in range(1, groups_y):
        part_copy(k).wait_recv()
    total = functools.reduce(jnp.add, [gathered[k] for k in range(groups_y - 1)], part_ref[tile_y])
    mine[...] = total
    samp_ref[tile_y] = total
    for k in range(1, groups_y):
        sum_copy(k, tile_y).start()
    piece(cuts[1], cuts[2], False)
    to_north.wait_recv()
    to_south.wait_recv()
    piece(cuts[2], cuts[3], True)
    for i in range(cuts[3], cells_x - 1):
        inside(i, True)

    @pl.when(tile_x > 0)
    def _():
        to_east.wait_recv()

    @pl.when(tile_x < last_x)
    def _():
        to_west.wait_recv()

    plane(
        0,
        lambda c, rows, lanes: x_recv[0, c, rows, lanes],
        lambda c, rows, lanes: field[c, 1, rows, lanes],
        True,
    )
    plane(
        cells_x - 1,
        lambda c, rows, lanes: field[c, cells_x - 2, rows, lanes],
        lambda c, rows, lanes: x_recv[1, c, rows, lanes],
        True,
    )

    @pl.loop(0, (cuts[2] - cuts[0]) // STEP)
    def _(n):
        for k in range(STEP):
            i = cuts[0] + n * STEP + k
            for side, t, mask in ((0, 0, first_row), (1, strips - 1, last_row)):
                rows = pl.ds(8 * t, 8)
                for half in range(2):
                    bv = b * tile(1, i, t, half)
                    weight = jnp.where(mask, a - bv if side else a + bv, 0.0)
                    for c in range(comps):
                        before = result[c, i, rows, halves[half]]
                        result[c, i, rows, halves[half]] = before + weight * ghost(side, half, c, i)

    for k in range(1, groups_y):
        sum_copy(k, peer(groups_y - k)).wait_recv()
    for k in range(1, groups_y):
        part_copy(k).wait_send()
        sum_copy(k, tile_y).wait_send()
    to_north.wait_send()
    to_south.wait_send()

    @pl.when(tile_x < last_x)
    def _():
        to_east.wait_send()

    @pl.when(tile_x > 0)
    def _():
        to_west.wait_send()


def local(groups_x, groups_y, velocity, inflow, positions, tiles, coefs, counts):
    comps, cells_x, cells_y, depth = velocity.shape
    total_y = cells_y * groups_y
    pos, tiles, coefs = positions[0].transpose(1, 0, 2), tiles[0].T, coefs[0]
    _, recs, points = pos.shape
    velocity, pos, tiles = (
        pltpu.with_memory_space_constraint(x, pltpu.HBM) for x in (velocity, pos, tiles)
    )
    grid = pltpu.VMEM(velocity.shape, F32)
    table = pltpu.VMEM((groups_y, comps, recs * points // (groups_y * LANES), LANES), F32)

    field, _, part, plan, picks, along = pl.pallas_call(
        functools.partial(sample_first, total_y, groups_y),
        out_shape=(
            grid,
            pltpu.VMEM(pos.shape, I32),
            table,
            pltpu.SMEM((8, LANES), I32),
            pltpu.VMEM((recs, depth, points), BF16),
            pltpu.VMEM((recs, cells_y, points), F32),
        ),
        in_specs=[HBM, HBM, HBM, SMEM],
        out_specs=(VMEM, VMEM, VMEM, SMEM, VMEM, VMEM),
        scratch_shapes=[
            pltpu.VMEM(tiles.shape, I32),
            pltpu.VMEM((8, LANES), I32),
            pltpu.SemaphoreType.DMA((CHUNKS + 3,)),
        ],
        compiler_params=params(),
        name="sample_first",
    )(velocity, pos, tiles, counts)

    def swap(second, *operands):
        sems = 2 * (groups_y - 1) + 4
        return pl.pallas_call(
            functools.partial(exchange, groups_x, groups_y, second),
            out_shape=(grid, table),
            in_specs=[VMEM] * len(operands),
            out_specs=(VMEM, VMEM),
            scratch_shapes=[
                pltpu.VMEM((2, 2, comps, cells_x, LANES), F32),
                pltpu.VMEM((2, 2, comps, cells_x, LANES), F32),
                pltpu.VMEM((2, comps, cells_y, depth), F32),
                pltpu.VMEM((groups_y - 1, *table.shape[1:]), F32),
                pltpu.VMEM(table.shape[1:], F32),
                pltpu.SemaphoreType.DMA((sems,)),
                pltpu.SemaphoreType.DMA((sems,)),
            ],
            compiler_params=params(collective_id=int(second), has_side_effects=True),
            name="exchange_second" if second else "exchange_first",
        )(*operands)

    section, samp_a = swap(False, field, part, inflow)
    section, part = pl.pallas_call(
        spread_and_sample,
        out_shape=(grid, table),
        in_specs=[SMEM] + [VMEM] * 5,
        out_specs=(VMEM, VMEM),
        input_output_aliases={5: 0},
        compiler_params=params(),
        name="spread_and_sample",
    )(plan, picks, along, coefs, samp_a, section)
    final, samp_b = swap(True, field, section, part, inflow)
    _, velocity_next, blade = pl.pallas_call(
        spread_last,
        out_shape=(
            grid,
            jax.ShapeDtypeStruct(velocity.shape, F32),
            jax.ShapeDtypeStruct(pos.shape, F32),
        ),
        in_specs=[SMEM, VMEM, VMEM, VMEM, SMEM, VMEM, VMEM, VMEM],
        out_specs=(VMEM, HBM, VMEM),
        input_output_aliases={7: 0},
        scratch_shapes=[pltpu.SemaphoreType.DMA((CHUNKS,))],
        compiler_params=params(),
        name="spread_last",
    )(plan, picks, along, coefs, counts, samp_a, samp_b, final)
    return (velocity_next, blade.transpose(1, 0, 2)[None])


def solution(mesh):
    return jax.shard_map(
        functools.partial(local, mesh.shape["gx"], mesh.shape["gy"]),
        mesh=mesh,
        in_specs=(
            P(None, "gx", "gy", None),
            P(None, "gy", None),
            P("gx", None, None, None),
            P("gx", None, None),
            P("gx", None, None),
            P("gx"),
        ),
        out_specs=(P(None, "gx", "gy", None), P("gx", None, None, None)),
        check_vma=False,
    )
```

```python
import functools
import math

import jax
import jax.numpy as jnp
from jax import lax
from jax.experimental import pallas as pl
from jax.experimental.pallas import tpu as pltpu
from jax.sharding import PartitionSpec as P

F32, BF16, I32 = jnp.float32, jnp.bfloat16, jnp.int32
RAD = 2
VISCOSITY = 0.05
TIME_STEP = 0.1
WIDTH_EPS = 1.5
K0, K1, K2 = (
    math.exp(-((d / WIDTH_EPS) ** 2)) / (WIDTH_EPS * math.sqrt(math.pi)) for d in range(3)
)
MESH = pl.DeviceIdType.MESH
VMEM = pl.BlockSpec(memory_space=pltpu.VMEM)
SMEM = pl.BlockSpec(memory_space=pltpu.SMEM)
HBM = pl.BlockSpec(memory_space=pltpu.HBM)
LANES = 128
STEP = 4
CHUNKS = 4


def params(**kw):
    return pltpu.CompilerParams(vmem_limit_bytes=6 << 20, **kw)


def local_y(pos_y, tile_y, cells_y, total_y):
    return lax.rem(pos_y - tile_y * cells_y + total_y + total_y // 2, total_y) - total_y // 2


def smooth_z(block):
    near = pltpu.roll(block, 1, 1) + pltpu.roll(block, block.shape[1] - 1, 1)
    far = pltpu.roll(block, 2, 1) + pltpu.roll(block, block.shape[1] - 2, 1)
    return K0 * block + K1 * near + K2 * far


def split_dot(block, pick, dims):
    rows = block.shape[0]
    high = block.astype(BF16)
    low = (block - high.astype(F32)).astype(BF16)
    both = lax.dot_general(
        jnp.concatenate([high, low], axis=0), pick, (dims, ((), ())), preferred_element_type=F32
    )
    return both[:rows] + both[rows:]


def build_tables(pos_ref, pick_ref, here_ref, n, rec, tile_y, cells_y, total_y):
    depth, points = pick_ref.shape[1:]
    cell = lax.broadcasted_iota(I32, (depth, points), 0)
    pick_ref[n] = (cell == pos_ref[2, pl.ds(rec, 1), :]).astype(F32).astype(BF16)
    here_ref[pl.ds(n, 1), :] = local_y(pos_ref[1, pl.ds(rec, 1), :], tile_y, cells_y, total_y)


def weight_y(here_ref, n, cells_y):
    here = here_ref[pl.ds(n, 1), :]
    dist = jnp.abs(lax.broadcasted_iota(I32, (cells_y, here.shape[1]), 0) - here)
    return jnp.where(
        dist == 0, K0, jnp.where(dist == 1, K1, jnp.where(dist == 2, K2, 0.0))
    ).astype(F32)


def sample_pair(field, plan_ref, pick_ref, here_ref, part_ref, pair, count):
    comps, _, cells_y, depth = field.shape
    for n in (2 * pair, jnp.minimum(2 * pair + 1, count - 1)):
        rec, hub = plan_ref[0, n], plan_ref[1, n]
        planes = (
            K0 * field[:, hub]
            + K1 * (field[:, hub - 1] + field[:, hub + 1])
            + K2 * (field[:, hub - 2] + field[:, hub + 2])
        )
        smooth = smooth_z(planes.reshape(comps * cells_y, depth))
        inner = split_dot(smooth, pick_ref[n], ((1,), (0,)))
        value = jnp.sum(inner.reshape(comps, cells_y, -1) * weight_y(here_ref, n, cells_y)[None], axis=1)
        group, row = rec // 8, lax.rem(rec, 8)
        for half in range(2):
            for c in range(comps):
                part_ref[half * 8 + group, c, pl.ds(row, 1), :] = value[
                    c : c + 1, half * LANES : (half + 1) * LANES
                ]


def spread_pair(field, plan_ref, pick_ref, here_ref, coef_ref, samp_ref, scale, pair, count):
    comps, _, cells_y, depth = field.shape
    slabs = []
    for k in range(2):
        n = jnp.minimum(2 * pair + k, count - 1)
        rec, hub = plan_ref[0, n], plan_ref[1, n]
        factor = jnp.where(2 * pair + k < count, -scale, 0.0)
        group, row = rec // 8, lax.rem(rec, 8)
        sampled = [
            jnp.concatenate(
                [samp_ref[half * 8 + group, c, pl.ds(row, 1), :] for half in range(2)], axis=1
            )
            for c in range(comps)
        ]
        speed = jnp.sqrt(sampled[0] * sampled[0] + sampled[1] * sampled[1] + sampled[2] * sampled[2])
        strength = coef_ref[pl.ds(rec, 1), :] * speed * factor
        along = weight_y(here_ref, n, cells_y)
        weighted = jnp.concatenate([along * (strength * value) for value in sampled], axis=0)
        slab = smooth_z(split_dot(weighted, pick_ref[n], ((1,), (1,))))
        slabs.append((hub, slab.reshape(comps, cells_y, depth)))
    for hub, slab in slabs:
        for d, weight in ((-2, K2), (-1, K1), (0, K0), (1, K1), (2, K2)):
            field[:, hub + d] += weight * slab


def make_plan(total_y, groups_y, pos_ref, tiles_ref, counts_ref, rows_ref, cells_x, cells_y):
    recs = pos_ref.shape[1]
    tile_x, tile_y = lax.axis_index("gx"), lax.axis_index("gy")
    rec = lax.broadcasted_iota(I32, (recs, LANES), 0)
    lane = lax.broadcasted_iota(I32, (recs, LANES), 1)
    square = lax.broadcasted_iota(I32, (recs, recs), 0) == lax.broadcasted_iota(I32, (recs, recs), 1)

    def column(row):
        return jnp.sum(jnp.where(square, row.astype(F32), 0.0), axis=1, keepdims=True).astype(I32)

    here = local_y(pos_ref[1], tile_y, cells_y, total_y)
    near = ((here >= -RAD) & (here < cells_y + RAD)).astype(I32)
    touched = jnp.max(near, axis=1, keepdims=True)
    hub = pos_ref[0, :, 0:1] - tile_x * cells_x
    first, number = column(tiles_ref[0:1, :]), column(tiles_ref[1:2, :])
    listed = lax.rem(tile_y - first + groups_y, groups_y) < number
    active = listed & (touched > 0) & (rec[:, 0:1] < counts_ref[0])
    big = jnp.int32(1 << 20)
    key = jnp.where(active, hub * recs + rec[:, 0:1], big)
    key_row = jnp.min(jnp.where(rec == lane, key, big), axis=0, keepdims=True)
    rank = jnp.sum((key_row < key).astype(F32), axis=1, keepdims=True).astype(I32)
    live = active.astype(F32)
    count = jnp.sum(live, axis=0, keepdims=True).astype(I32)
    mine = active & (rank == jnp.minimum(lane, count - 1))
    rows_ref[0:1, :] = jnp.sum(jnp.where(mine, rec, 0).astype(F32), axis=0, keepdims=True).astype(I32)
    rows_ref[1:2, :] = jnp.sum(jnp.where(mine, hub, 0).astype(F32), axis=0, keepdims=True).astype(I32)
    below = active & (hub < lane)
    rows_ref[2:3, :] = jnp.sum(below.astype(F32), axis=0, keepdims=True).astype(I32)


def sample_first(total_y, groups_y, vel_hbm, pos_hbm, tiles_hbm, counts_ref,
                 field, pos_ref, part_ref, plan_ref, pick_ref, here_ref, tiles_ref, rows_ref, sems):
    cells_x, cells_y = field.shape[1:3]
    tile_y = lax.axis_index("gy")
    chunk = cells_x // CHUNKS
    fetch_pos = pltpu.make_async_copy(pos_hbm, pos_ref, sems.at[CHUNKS])
    fetch_tiles = pltpu.make_async_copy(tiles_hbm, tiles_ref, sems.at[CHUNKS + 1])
    fetch_pos.start()
    fetch_tiles.start()
    loads = []
    for q in range(CHUNKS):
        planes = pl.ds(q * chunk, chunk)
        loads.append(pltpu.make_async_copy(vel_hbm.at[:, planes], field.at[:, planes], sems.at[q]))
        loads[-1].start()
    part_ref[...] = jnp.zeros_like(part_ref)
    rows_ref[...] = jnp.zeros_like(rows_ref)
    fetch_pos.wait()
    fetch_tiles.wait()
    make_plan(total_y, groups_y, pos_ref, tiles_ref, counts_ref, rows_ref, cells_x, cells_y)
    fetch_plan = pltpu.make_async_copy(rows_ref, plan_ref, sems.at[CHUNKS + 2])
    fetch_plan.start()
    fetch_plan.wait()
    count = plan_ref[2, LANES - 1]

    @pl.loop(0, count)
    def _(n):
        build_tables(pos_ref, pick_ref, here_ref, n, plan_ref[0, n], tile_y, cells_y, total_y)

    start = jnp.int32(0)
    for q in range(CHUNKS):
        loads[q].wait()
        if q < CHUNKS - 1:
            stop = plan_ref[2, (q + 1) * chunk - RAD] // 2
        else:
            stop = (count + 1) // 2

        @pl.loop(start, stop)
        def _(pair):
            sample_pair(field, plan_ref, pick_ref, here_ref, part_ref, pair, count)

        start = stop


def spread_and_sample(plan_ref, pick_ref, here_ref, coef_ref, samp_ref, _, field, part_ref):
    count = plan_ref[2, LANES - 1]
    part_ref[...] = jnp.zeros_like(part_ref)

    @pl.loop(0, (count + 1) // 2)
    def _(pair):
        spread_pair(field, plan_ref, pick_ref, here_ref, coef_ref, samp_ref, TIME_STEP, pair, count)

    @pl.loop(0, (count + 1) // 2)
    def _(pair):
        sample_pair(field, plan_ref, pick_ref, here_ref, part_ref, pair, count)


def spread_last(plan_ref, pick_ref, here_ref, coef_ref, counts_ref, samp_a, samp_b, _,
                field, next_hbm, blade_hbm, blade, sems):
    comps, recs, _ = blade.shape
    chunk = field.shape[1] // CHUNKS
    count = plan_ref[2, LANES - 1]
    for half in range(2):
        lanes = pl.ds(half * LANES, LANES)
        for group in range(recs // 8):
            rows = pl.ds(group * 8, 8)
            a = [samp_a[half * 8 + group, c] for c in range(comps)]
            b = [samp_b[half * 8 + group, c] for c in range(comps)]
            speed_a = jnp.sqrt(a[0] * a[0] + a[1] * a[1] + a[2] * a[2])
            speed_b = jnp.sqrt(b[0] * b[0] + b[1] * b[1] + b[2] * b[2])
            rec = group * 8 + lax.broadcasted_iota(I32, (8, LANES), 0)
            strength = jnp.where(rec < counts_ref[0], coef_ref[rows, lanes] * -0.5, 0.0)
            for c in range(comps):
                blade[c, rows, lanes] = strength * (speed_a * a[c] + speed_b * b[c])
    put = pltpu.make_async_copy(blade, blade_hbm, sems.at[CHUNKS])
    put.start()
    start = jnp.int32(0)
    stores = []
    for q in range(CHUNKS):
        if q < CHUNKS - 1:
            stop = (plan_ref[2, (q + 1) * chunk + RAD] + 1) // 2
        else:
            stop = (count + 1) // 2

        @pl.loop(start, stop)
        def _(pair):
            spread_pair(field, plan_ref, pick_ref, here_ref, coef_ref, samp_b,
                        0.5 * TIME_STEP, pair, count)

        planes = pl.ds(q * chunk, chunk)
        stores.append(pltpu.make_async_copy(field.at[:, planes], next_hbm.at[:, planes], sems.at[q]))
        stores[-1].start()
        start = stop

    for store in stores:
        store.wait()
    put.wait()


def exchange(groups_x, groups_y, second, *refs):
    if second:
        old, refs = refs[0], refs[1:]
    (field, part_ref, inflow, result, samp_ref,
     y_send, y_recv, x_recv, gathered, mine, send_sem, recv_sem) = refs
    comps, cells_x, cells_y, depth = field.shape
    tile_x, tile_y = lax.axis_index("gx"), lax.axis_index("gy")
    last_x = groups_x - 1

    def peer(k):
        return lax.rem(tile_y + k, groups_y)

    north, south = peer(1), peer(groups_y - 1)
    barrier = pltpu.get_barrier_semaphore()
    for k in range(1, groups_y):
        pl.semaphore_signal(barrier, inc=1, device_id={"gy": peer(k)}, device_id_type=MESH)

    @pl.when(tile_x > 0)
    def _():
        pl.semaphore_signal(barrier, inc=1, device_id={"gx": tile_x - 1}, device_id_type=MESH)

    @pl.when(tile_x < last_x)
    def _():
        pl.semaphore_signal(barrier, inc=1, device_id={"gx": tile_x + 1}, device_id_type=MESH)

    @pl.loop(0, cells_x // 8)
    def _(block):
        rows = pl.ds(block * 8, 8)
        for c in range(comps):
            for half in range(2):
                lanes = pl.ds(half * LANES, LANES)
                y_send[0, half, c, rows, :] = field[c, rows, 0, lanes]
                y_send[1, half, c, rows, :] = field[c, rows, cells_y - 1, lanes]

    @pl.when(tile_x == 0)
    def _():
        x_recv[0] = inflow[...]

    @pl.when(tile_x == last_x)
    def _():
        x_recv[1] = field[:, cells_x - 1]

    neighbours = (tile_x > 0).astype(I32) + (tile_x < last_x).astype(I32)
    pl.semaphore_wait(barrier, groups_y - 1 + neighbours)

    def remote(src, dst, slot, where):
        return pltpu.make_async_remote_copy(
            src_ref=src, dst_ref=dst, send_sem=send_sem.at[slot], recv_sem=recv_sem.at[slot],
            device_id=where, device_id_type=MESH,
        )

    def part_copy(k):
        return remote(part_ref.at[peer(k)], gathered.at[k - 1], k - 1, {"gy": peer(k)})

    def sum_copy(k, owner):
        return remote(mine, samp_ref.at[owner], groups_y + k - 2, {"gy": peer(k)})

    base = groups_y - 1
    to_north = remote(y_send.at[1], y_recv.at[0], 2 * base, {"gy": north})
    to_south = remote(y_send.at[0], y_recv.at[1], 2 * base + 1, {"gy": south})
    to_east = remote(field.at[:, cells_x - 1], x_recv.at[0], 2 * base + 2, {"gx": tile_x + 1})
    to_west = remote(field.at[:, 0], x_recv.at[1], 2 * base + 3, {"gx": tile_x - 1})

    for k in range(1, groups_y):
        part_copy(k).start()
    to_north.start()
    to_south.start()

    @pl.when(tile_x < last_x)
    def _():
        to_east.start()

    @pl.when(tile_x > 0)
    def _():
        to_west.start()

    scale = 0.5 if second else 1.0
    a = scale * TIME_STEP * VISCOSITY
    b = scale * TIME_STEP * 0.5
    centre = scale * (1.0 - 6.0 * TIME_STEP * VISCOSITY)
    sub = lax.broadcasted_iota(I32, (8, LANES), 0)
    lane = lax.broadcasted_iota(I32, (8, LANES), 1)
    first_row, last_row = sub == 0, sub == 7
    first_lane, last_lane = lane == 0, lane == LANES - 1
    zero = jnp.zeros((8, LANES), F32)
    halves = [pl.ds(half * LANES, LANES) for half in range(2)]
    strips = cells_y // 8

    def tile(c, i, t, half):
        return field[c, i, pl.ds(8 * t, 8), halves[half]]

    def ghost(side, half, c, i):
        return y_recv[side, half, c, pl.ds(i, 8, stride=0), :]

    def plane(i, west, east, ghosts):
        for t in range(strips):
            rows = pl.ds(8 * t, 8)
            here = [[tile(c, i, t, half) for half in range(2)] for c in range(comps)]
            lower, upper = [], []
            for c in range(comps):
                up = [pltpu.roll(v, 1, 1) for v in here[c]]
                down = [pltpu.roll(v, LANES - 1, 1) for v in here[c]]
                lower.append([jnp.where(first_lane, zero, up[0]), jnp.where(first_lane, up[0], up[1])])
                upper.append([jnp.where(last_lane, down[1], down[0]), jnp.where(last_lane, zero, down[1])])
            for half in range(2):
                bu, bv, bw = (b * here[c][half] for c in range(3))
                for c in range(comps):
                    if t > 0:
                        below = pltpu.roll(tile(c, i, t - 1, half), 1, 0)
                    else:
                        below = ghost(0, half, c, i) if ghosts else zero
                    if t < strips - 1:
                        above = pltpu.roll(tile(c, i, t + 1, half), 7, 0)
                    else:
                        above = ghost(1, half, c, i) if ghosts else zero
                    value = here[c][half]
                    to_s = jnp.where(first_row, below, pltpu.roll(value, 1, 0))
                    to_n = jnp.where(last_row, above, pltpu.roll(value, 7, 0))
                    out = (
                        centre * value
                        + ((a - bu) * east(c, rows, halves[half]) + (a + bu) * west(c, rows, halves[half]))
                        + ((a - bv) * to_n + (a + bv) * to_s)
                        + ((a - bw) * upper[c][half] + (a + bw) * lower[c][half])
                    )
                    if second:
                        out = out + 0.5 * old[c, i, rows, halves[half]]
                    result[c, i, rows, halves[half]] = out

    def inside(i, ghosts):
        plane(
            i,
            lambda c, rows, lanes: field[c, i - 1, rows, lanes],
            lambda c, rows, lanes: field[c, i + 1, rows, lanes],
            ghosts,
        )

    def piece(start, stop, ghosts):
        @pl.loop(0, (stop - start) // STEP)
        def _(n):
            for k in range(STEP):
                inside(start + n * STEP + k, ghosts)

    steps = (cells_x - 2) // STEP
    cuts = [1 + STEP * (steps * k // 4) for k in (0, 2, 3, 4)]

    piece(cuts[0], cuts[1], False)
    for k in range(1, groups_y):
        part_copy(k).wait_recv()
    total = functools.reduce(jnp.add, [gathered[k] for k in range(groups_y - 1)], part_ref[tile_y])
    mine[...] = total
    samp_ref[tile_y] = total
    for k in range(1, groups_y):
        sum_copy(k, tile_y).start()
    piece(cuts[1], cuts[2], False)
    to_north.wait_recv()
    to_south.wait_recv()
    piece(cuts[2], cuts[3], True)
    for i in range(cuts[3], cells_x - 1):
        inside(i, True)

    @pl.when(tile_x > 0)
    def _():
        to_east.wait_recv()

    @pl.when(tile_x < last_x)
    def _():
        to_west.wait_recv()

    plane(
        0,
        lambda c, rows, lanes: x_recv[0, c, rows, lanes],
        lambda c, rows, lanes: field[c, 1, rows, lanes],
        True,
    )
    plane(
        cells_x - 1,
        lambda c, rows, lanes: field[c, cells_x - 2, rows, lanes],
        lambda c, rows, lanes: x_recv[1, c, rows, lanes],
        True,
    )

    @pl.loop(0, (cuts[2] - cuts[0]) // STEP)
    def _(n):
        for k in range(STEP):
            i = cuts[0] + n * STEP + k
            for side, t, mask in ((0, 0, first_row), (1, strips - 1, last_row)):
                rows = pl.ds(8 * t, 8)
                for half in range(2):
                    bv = b * tile(1, i, t, half)
                    weight = jnp.where(mask, a - bv if side else a + bv, 0.0)
                    for c in range(comps):
                        before = result[c, i, rows, halves[half]]
                        result[c, i, rows, halves[half]] = before + weight * ghost(side, half, c, i)

    for k in range(1, groups_y):
        sum_copy(k, peer(groups_y - k)).wait_recv()
    for k in range(1, groups_y):
        part_copy(k).wait_send()
        sum_copy(k, tile_y).wait_send()
    to_north.wait_send()
    to_south.wait_send()

    @pl.when(tile_x < last_x)
    def _():
        to_east.wait_send()

    @pl.when(tile_x > 0)
    def _():
        to_west.wait_send()


def local(groups_x, groups_y, velocity, inflow, positions, tiles, coefs, counts):
    comps, cells_x, cells_y, depth = velocity.shape
    total_y = cells_y * groups_y
    pos, tiles, coefs = positions[0].transpose(1, 0, 2), tiles[0].T, coefs[0]
    _, recs, points = pos.shape
    velocity, pos, tiles = (
        pltpu.with_memory_space_constraint(x, pltpu.HBM) for x in (velocity, pos, tiles)
    )
    grid = pltpu.VMEM(velocity.shape, F32)
    table = pltpu.VMEM((groups_y, comps, recs * points // (groups_y * LANES), LANES), F32)

    field, _, part, plan, picks, here = pl.pallas_call(
        functools.partial(sample_first, total_y, groups_y),
        out_shape=(
            grid,
            pltpu.VMEM(pos.shape, I32),
            table,
            pltpu.SMEM((8, LANES), I32),
            pltpu.VMEM((recs, depth, points), BF16),
            pltpu.VMEM((recs, points), I32),
        ),
        in_specs=[HBM, HBM, HBM, SMEM],
        out_specs=(VMEM, VMEM, VMEM, SMEM, VMEM, VMEM),
        scratch_shapes=[
            pltpu.VMEM(tiles.shape, I32),
            pltpu.VMEM((8, LANES), I32),
            pltpu.SemaphoreType.DMA((CHUNKS + 3,)),
        ],
        compiler_params=params(),
        name="sample_first",
    )(velocity, pos, tiles, counts)

    def swap(second, *operands):
        sems = 2 * (groups_y - 1) + 4
        return pl.pallas_call(
            functools.partial(exchange, groups_x, groups_y, second),
            out_shape=(grid, table),
            in_specs=[VMEM] * len(operands),
            out_specs=(VMEM, VMEM),
            scratch_shapes=[
                pltpu.VMEM((2, 2, comps, cells_x, LANES), F32),
                pltpu.VMEM((2, 2, comps, cells_x, LANES), F32),
                pltpu.VMEM((2, comps, cells_y, depth), F32),
                pltpu.VMEM((groups_y - 1, *table.shape[1:]), F32),
                pltpu.VMEM(table.shape[1:], F32),
                pltpu.SemaphoreType.DMA((sems,)),
                pltpu.SemaphoreType.DMA((sems,)),
            ],
            compiler_params=params(collective_id=int(second), has_side_effects=True),
            name="exchange_second" if second else "exchange_first",
        )(*operands)

    section, samp_a = swap(False, field, part, inflow)
    section, part = pl.pallas_call(
        spread_and_sample,
        out_shape=(grid, table),
        in_specs=[SMEM] + [VMEM] * 5,
        out_specs=(VMEM, VMEM),
        input_output_aliases={5: 0},
        compiler_params=params(),
        name="spread_and_sample",
    )(plan, picks, here, coefs, samp_a, section)
    final, samp_b = swap(True, field, section, part, inflow)
    _, velocity_next, blade = pl.pallas_call(
        spread_last,
        out_shape=(
            grid,
            jax.ShapeDtypeStruct(velocity.shape, F32),
            jax.ShapeDtypeStruct(pos.shape, F32),
        ),
        in_specs=[SMEM, VMEM, VMEM, VMEM, SMEM, VMEM, VMEM, VMEM],
        out_specs=(VMEM, HBM, HBM),
        input_output_aliases={7: 0},
        scratch_shapes=[pltpu.VMEM(pos.shape, F32), pltpu.SemaphoreType.DMA((CHUNKS + 1,))],
        compiler_params=params(),
        name="spread_last",
    )(plan, picks, here, coefs, counts, samp_a, samp_b, final)
    return (velocity_next, blade.transpose(1, 0, 2)[None])


def solution(mesh):
    return jax.shard_map(
        functools.partial(local, mesh.shape["gx"], mesh.shape["gy"]),
        mesh=mesh,
        in_specs=(
            P(None, "gx", "gy", None),
            P(None, "gy", None),
            P("gx", None, None, None),
            P("gx", None, None),
            P("gx", None, None),
            P("gx"),
        ),
        out_specs=(P(None, "gx", "gy", None), P("gx", None, None, None)),
        check_vma=False,
    )
```

```python
import functools
import math

import jax
import jax.numpy as jnp
from jax import lax
from jax.experimental import pallas as pl
from jax.experimental.pallas import tpu as pltpu
from jax.sharding import PartitionSpec as P

F32, BF16, I32 = jnp.float32, jnp.bfloat16, jnp.int32
RAD = 2
VISCOSITY = 0.05
TIME_STEP = 0.1
WIDTH_EPS = 1.5
K0, K1, K2 = (
    math.exp(-((d / WIDTH_EPS) ** 2)) / (WIDTH_EPS * math.sqrt(math.pi)) for d in range(3)
)
MESH = pl.DeviceIdType.MESH
VMEM = pl.BlockSpec(memory_space=pltpu.VMEM)
SMEM = pl.BlockSpec(memory_space=pltpu.SMEM)
HBM = pl.BlockSpec(memory_space=pltpu.HBM)
LANES = 128
GROUP = 4
STEP = 4
CHUNKS = 4


def params(**kw):
    return pltpu.CompilerParams(vmem_limit_bytes=6 << 20, **kw)


def local_y(pos_y, tile_y, cells_y, total_y):
    return lax.rem(pos_y - tile_y * cells_y + total_y + total_y // 2, total_y) - total_y // 2


def smooth_z(block):
    near = pltpu.roll(block, 1, 1) + pltpu.roll(block, block.shape[1] - 1, 1)
    far = pltpu.roll(block, 2, 1) + pltpu.roll(block, block.shape[1] - 2, 1)
    return K0 * block + K1 * near + K2 * far


def split_dot(block, pick, dims):
    rows = block.shape[0]
    high = block.astype(BF16)
    low = (block - high.astype(F32)).astype(BF16)
    both = lax.dot_general(
        jnp.concatenate([high, low], axis=0), pick, (dims, ((), ())), preferred_element_type=F32
    )
    return both[:rows] + both[rows:]


def build_tables(pos_ref, pick_ref, here_ref, n, rec, tile_y, cells_y, total_y):
    depth, points = pick_ref.shape[1:]
    cell = lax.broadcasted_iota(I32, (depth, points), 0)
    pick_ref[n] = (cell == pos_ref[2, pl.ds(rec, 1), :]).astype(F32).astype(BF16)
    here_ref[pl.ds(n, 1), :] = local_y(pos_ref[1, pl.ds(rec, 1), :], tile_y, cells_y, total_y)


def weight_y(here_ref, n, cells_y):
    here = here_ref[pl.ds(n, 1), :]
    dist = jnp.abs(lax.broadcasted_iota(I32, (cells_y, here.shape[1]), 0) - here)
    return jnp.where(
        dist == 0, K0, jnp.where(dist == 1, K1, jnp.where(dist == 2, K2, 0.0))
    ).astype(F32)


def sample_group(size, field, plan_ref, pick_ref, here_ref, part_ref, group_at, count):
    comps, _, cells_y, depth = field.shape
    for k in range(size):
        n = jnp.minimum(size * group_at + k, count - 1)
        rec, hub = plan_ref[0, n], plan_ref[1, n]
        planes = (
            K0 * field[:, hub]
            + K1 * (field[:, hub - 1] + field[:, hub + 1])
            + K2 * (field[:, hub - 2] + field[:, hub + 2])
        )
        smooth = smooth_z(planes.reshape(comps * cells_y, depth))
        inner = split_dot(smooth, pick_ref[n], ((1,), (0,)))
        value = jnp.sum(inner.reshape(comps, cells_y, -1) * weight_y(here_ref, n, cells_y)[None], axis=1)
        group, row = rec // 8, lax.rem(rec, 8)
        for half in range(2):
            for c in range(comps):
                part_ref[half * 8 + group, c, pl.ds(row, 1), :] = value[
                    c : c + 1, half * LANES : (half + 1) * LANES
                ]


def spread_group(size, field, plan_ref, pick_ref, here_ref, coef_ref, samp_ref, scale, group_at, count):
    comps, _, cells_y, depth = field.shape
    slabs = []
    for k in range(size):
        n = jnp.minimum(size * group_at + k, count - 1)
        rec, hub = plan_ref[0, n], plan_ref[1, n]
        factor = jnp.where(size * group_at + k < count, -scale, 0.0)
        group, row = rec // 8, lax.rem(rec, 8)
        sampled = [
            jnp.concatenate(
                [samp_ref[half * 8 + group, c, pl.ds(row, 1), :] for half in range(2)], axis=1
            )
            for c in range(comps)
        ]
        speed = jnp.sqrt(sampled[0] * sampled[0] + sampled[1] * sampled[1] + sampled[2] * sampled[2])
        strength = coef_ref[pl.ds(rec, 1), :] * speed * factor
        along = weight_y(here_ref, n, cells_y)
        weighted = jnp.concatenate([along * (strength * value) for value in sampled], axis=0)
        slab = smooth_z(split_dot(weighted, pick_ref[n], ((1,), (1,))))
        slabs.append((hub, slab.reshape(comps, cells_y, depth)))
    for hub, slab in slabs:
        for d, weight in ((-2, K2), (-1, K1), (0, K0), (1, K1), (2, K2)):
            field[:, hub + d] += weight * slab


def make_plan(total_y, groups_y, pos_ref, tiles_ref, counts_ref, rows_ref, cells_x, cells_y):
    recs = pos_ref.shape[1]
    tile_x, tile_y = lax.axis_index("gx"), lax.axis_index("gy")
    rec = lax.broadcasted_iota(I32, (recs, LANES), 0)
    lane = lax.broadcasted_iota(I32, (recs, LANES), 1)
    square = lax.broadcasted_iota(I32, (recs, recs), 0) == lax.broadcasted_iota(I32, (recs, recs), 1)

    def column(row):
        return jnp.sum(jnp.where(square, row.astype(F32), 0.0), axis=1, keepdims=True).astype(I32)

    here = local_y(pos_ref[1], tile_y, cells_y, total_y)
    near = ((here >= -RAD) & (here < cells_y + RAD)).astype(I32)
    touched = jnp.max(near, axis=1, keepdims=True)
    hub = pos_ref[0, :, 0:1] - tile_x * cells_x
    first, number = column(tiles_ref[0:1, :]), column(tiles_ref[1:2, :])
    listed = lax.rem(tile_y - first + groups_y, groups_y) < number
    active = listed & (touched > 0) & (rec[:, 0:1] < counts_ref[0])
    big = jnp.int32(1 << 20)
    key = jnp.where(active, hub * recs + rec[:, 0:1], big)
    key_row = jnp.min(jnp.where(rec == lane, key, big), axis=0, keepdims=True)
    rank = jnp.sum((key_row < key).astype(F32), axis=1, keepdims=True).astype(I32)
    live = active.astype(F32)
    count = jnp.sum(live, axis=0, keepdims=True).astype(I32)
    mine = active & (rank == jnp.minimum(lane, count - 1))
    rows_ref[0:1, :] = jnp.sum(jnp.where(mine, rec, 0).astype(F32), axis=0, keepdims=True).astype(I32)
    rows_ref[1:2, :] = jnp.sum(jnp.where(mine, hub, 0).astype(F32), axis=0, keepdims=True).astype(I32)
    below = active & (hub < lane)
    rows_ref[2:3, :] = jnp.sum(below.astype(F32), axis=0, keepdims=True).astype(I32)


def sample_first(total_y, groups_y, vel_hbm, pos_hbm, tiles_hbm, counts_ref,
                 field, pos_ref, part_ref, plan_ref, pick_ref, here_ref, tiles_ref, rows_ref, sems):
    cells_x, cells_y = field.shape[1:3]
    tile_y = lax.axis_index("gy")
    chunk = cells_x // CHUNKS
    fetch_pos = pltpu.make_async_copy(pos_hbm, pos_ref, sems.at[CHUNKS])
    fetch_tiles = pltpu.make_async_copy(tiles_hbm, tiles_ref, sems.at[CHUNKS + 1])
    fetch_pos.start()
    fetch_tiles.start()
    loads = []
    for q in range(CHUNKS):
        planes = pl.ds(q * chunk, chunk)
        loads.append(pltpu.make_async_copy(vel_hbm.at[:, planes], field.at[:, planes], sems.at[q]))
        loads[-1].start()
    part_ref[...] = jnp.zeros_like(part_ref)
    rows_ref[...] = jnp.zeros_like(rows_ref)
    fetch_pos.wait()
    fetch_tiles.wait()
    make_plan(total_y, groups_y, pos_ref, tiles_ref, counts_ref, rows_ref, cells_x, cells_y)
    fetch_plan = pltpu.make_async_copy(rows_ref, plan_ref, sems.at[CHUNKS + 2])
    fetch_plan.start()
    fetch_plan.wait()
    count = plan_ref[2, LANES - 1]

    @pl.loop(0, count)
    def _(n):
        build_tables(pos_ref, pick_ref, here_ref, n, plan_ref[0, n], tile_y, cells_y, total_y)

    def sample(size):
        def body(at):
            sample_group(size, field, plan_ref, pick_ref, here_ref, part_ref, at, count)

        return body

    start = jnp.int32(0)
    for q in range(CHUNKS):
        loads[q].wait()
        stop = (count if q == CHUNKS - 1 else plan_ref[2, (q + 1) * chunk - RAD]) // GROUP
        pl.loop(start, stop)(sample(GROUP))
        start = stop
    pl.loop(start * (GROUP // 2), (count + 1) // 2)(sample(2))


def spread_and_sample(plan_ref, pick_ref, here_ref, coef_ref, samp_ref, _, field, part_ref):
    count = plan_ref[2, LANES - 1]
    part_ref[...] = jnp.zeros_like(part_ref)

    def spread(size):
        def body(at):
            spread_group(size, field, plan_ref, pick_ref, here_ref, coef_ref, samp_ref, TIME_STEP,
                         at, count)

        return body

    def sample(size):
        def body(at):
            sample_group(size, field, plan_ref, pick_ref, here_ref, part_ref, at, count)

        return body

    full = count // GROUP
    for step in (spread, sample):
        pl.loop(0, full)(step(GROUP))
        pl.loop(full * (GROUP // 2), (count + 1) // 2)(step(2))


def spread_last(plan_ref, pick_ref, here_ref, coef_ref, counts_ref, samp_a, samp_b, _,
                field, next_hbm, blade_hbm, blade, sems):
    comps, recs, _ = blade.shape
    chunk = field.shape[1] // CHUNKS
    count = plan_ref[2, LANES - 1]
    for half in range(2):
        lanes = pl.ds(half * LANES, LANES)
        for group in range(recs // 8):
            rows = pl.ds(group * 8, 8)
            a = [samp_a[half * 8 + group, c] for c in range(comps)]
            b = [samp_b[half * 8 + group, c] for c in range(comps)]
            speed_a = jnp.sqrt(a[0] * a[0] + a[1] * a[1] + a[2] * a[2])
            speed_b = jnp.sqrt(b[0] * b[0] + b[1] * b[1] + b[2] * b[2])
            rec = group * 8 + lax.broadcasted_iota(I32, (8, LANES), 0)
            strength = jnp.where(rec < counts_ref[0], coef_ref[rows, lanes] * -0.5, 0.0)
            for c in range(comps):
                blade[c, rows, lanes] = strength * (speed_a * a[c] + speed_b * b[c])
    put = pltpu.make_async_copy(blade, blade_hbm, sems.at[CHUNKS])
    put.start()
    start = jnp.int32(0)
    stores = []
    for q in range(CHUNKS):
        upto = count if q == CHUNKS - 1 else plan_ref[2, (q + 1) * chunk + RAD]
        stop = (upto + GROUP - 1) // GROUP

        @pl.loop(start, stop)
        def _(at):
            spread_group(GROUP, field, plan_ref, pick_ref, here_ref, coef_ref, samp_b,
                         0.5 * TIME_STEP, at, count)

        planes = pl.ds(q * chunk, chunk)
        stores.append(pltpu.make_async_copy(field.at[:, planes], next_hbm.at[:, planes], sems.at[q]))
        stores[-1].start()
        start = stop

    for store in stores:
        store.wait()
    put.wait()


def exchange(groups_x, groups_y, second, *refs):
    if second:
        old, refs = refs[0], refs[1:]
    (field, part_ref, inflow, result, samp_ref,
     y_send, y_recv, x_recv, gathered, mine, send_sem, recv_sem) = refs
    comps, cells_x, cells_y, depth = field.shape
    tile_x, tile_y = lax.axis_index("gx"), lax.axis_index("gy")
    last_x = groups_x - 1

    def peer(k):
        return lax.rem(tile_y + k, groups_y)

    north, south = peer(1), peer(groups_y - 1)
    barrier = pltpu.get_barrier_semaphore()
    for k in range(1, groups_y):
        pl.semaphore_signal(barrier, inc=1, device_id={"gy": peer(k)}, device_id_type=MESH)

    @pl.when(tile_x > 0)
    def _():
        pl.semaphore_signal(barrier, inc=1, device_id={"gx": tile_x - 1}, device_id_type=MESH)

    @pl.when(tile_x < last_x)
    def _():
        pl.semaphore_signal(barrier, inc=1, device_id={"gx": tile_x + 1}, device_id_type=MESH)

    @pl.loop(0, cells_x // 8)
    def _(block):
        rows = pl.ds(block * 8, 8)
        for c in range(comps):
            for half in range(2):
                lanes = pl.ds(half * LANES, LANES)
                y_send[0, half, c, rows, :] = field[c, rows, 0, lanes]
                y_send[1, half, c, rows, :] = field[c, rows, cells_y - 1, lanes]

    @pl.when(tile_x == 0)
    def _():
        x_recv[0] = inflow[...]

    @pl.when(tile_x == last_x)
    def _():
        x_recv[1] = field[:, cells_x - 1]

    neighbours = (tile_x > 0).astype(I32) + (tile_x < last_x).astype(I32)
    pl.semaphore_wait(barrier, groups_y - 1 + neighbours)

    def remote(src, dst, slot, where):
        return pltpu.make_async_remote_copy(
            src_ref=src, dst_ref=dst, send_sem=send_sem.at[slot], recv_sem=recv_sem.at[slot],
            device_id=where, device_id_type=MESH,
        )

    def part_copy(k):
        return remote(part_ref.at[peer(k)], gathered.at[k - 1], k - 1, {"gy": peer(k)})

    def sum_copy(k, owner):
        return remote(mine, samp_ref.at[owner], groups_y + k - 2, {"gy": peer(k)})

    base = groups_y - 1
    chunk = cells_x // CHUNKS

    def y_copy(q, side):
        rows = pl.ds(q * chunk, chunk)
        return remote(y_send.at[1 - side, :, :, rows, :], y_recv.at[side, :, :, rows, :],
                      2 * base + 2 + 2 * q + side, {"gy": south if side else north})

    to_east = remote(field.at[:, cells_x - 1], x_recv.at[0], 2 * base, {"gx": tile_x + 1})
    to_west = remote(field.at[:, 0], x_recv.at[1], 2 * base + 1, {"gx": tile_x - 1})

    for k in range(1, groups_y):
        part_copy(k).start()
    for q in range(CHUNKS):
        for side in range(2):
            y_copy(q, side).start()

    @pl.when(tile_x < last_x)
    def _():
        to_east.start()

    @pl.when(tile_x > 0)
    def _():
        to_west.start()

    scale = 0.5 if second else 1.0
    a = scale * TIME_STEP * VISCOSITY
    b = scale * TIME_STEP * 0.5
    centre = scale * (1.0 - 6.0 * TIME_STEP * VISCOSITY)
    sub = lax.broadcasted_iota(I32, (8, LANES), 0)
    lane = lax.broadcasted_iota(I32, (8, LANES), 1)
    first_row, last_row = sub == 0, sub == 7
    first_lane, last_lane = lane == 0, lane == LANES - 1
    zero = jnp.zeros((8, LANES), F32)
    halves = [pl.ds(half * LANES, LANES) for half in range(2)]
    strips = cells_y // 8

    def tile(c, i, t, half):
        return field[c, i, pl.ds(8 * t, 8), halves[half]]

    def ghost(side, half, c, i):
        return y_recv[side, half, c, pl.ds(i, 8, stride=0), :]

    def plane(i, west, east):
        for t in range(strips):
            rows = pl.ds(8 * t, 8)
            here = [[tile(c, i, t, half) for half in range(2)] for c in range(comps)]
            lower, upper = [], []
            for c in range(comps):
                up = [pltpu.roll(v, 1, 1) for v in here[c]]
                down = [pltpu.roll(v, LANES - 1, 1) for v in here[c]]
                lower.append([jnp.where(first_lane, zero, up[0]), jnp.where(first_lane, up[0], up[1])])
                upper.append([jnp.where(last_lane, down[1], down[0]), jnp.where(last_lane, zero, down[1])])
            for half in range(2):
                bu, bv, bw = (b * here[c][half] for c in range(3))
                for c in range(comps):
                    if t > 0:
                        below = pltpu.roll(tile(c, i, t - 1, half), 1, 0)
                    else:
                        below = zero
                    if t < strips - 1:
                        above = pltpu.roll(tile(c, i, t + 1, half), 7, 0)
                    else:
                        above = zero
                    value = here[c][half]
                    to_s = jnp.where(first_row, below, pltpu.roll(value, 1, 0))
                    to_n = jnp.where(last_row, above, pltpu.roll(value, 7, 0))
                    out = (
                        centre * value
                        + ((a - bu) * east(c, rows, halves[half]) + (a + bu) * west(c, rows, halves[half]))
                        + ((a - bv) * to_n + (a + bv) * to_s)
                        + ((a - bw) * upper[c][half] + (a + bw) * lower[c][half])
                    )
                    if second:
                        out = out + 0.5 * old[c, i, rows, halves[half]]
                    result[c, i, rows, halves[half]] = out

    def inside(i):
        plane(
            i,
            lambda c, rows, lanes: field[c, i - 1, rows, lanes],
            lambda c, rows, lanes: field[c, i + 1, rows, lanes],
        )

    def piece(start, stop):
        @pl.loop(0, (stop - start) // STEP)
        def _(n):
            for k in range(STEP):
                inside(start + n * STEP + k)

    steps = (cells_x - 2) // STEP
    cuts = [1 + STEP * (steps * k // 4) for k in (0, 2, 4)]

    piece(cuts[0], cuts[1])
    for k in range(1, groups_y):
        part_copy(k).wait_recv()
    total = functools.reduce(jnp.add, [gathered[k] for k in range(groups_y - 1)], part_ref[tile_y])
    mine[...] = total
    samp_ref[tile_y] = total
    for k in range(1, groups_y):
        sum_copy(k, tile_y).start()
    piece(cuts[1], cuts[2])
    for i in range(cuts[2], cells_x - 1):
        inside(i)

    @pl.when(tile_x > 0)
    def _():
        to_east.wait_recv()

    @pl.when(tile_x < last_x)
    def _():
        to_west.wait_recv()

    plane(
        0,
        lambda c, rows, lanes: x_recv[0, c, rows, lanes],
        lambda c, rows, lanes: field[c, 1, rows, lanes],
    )
    plane(
        cells_x - 1,
        lambda c, rows, lanes: field[c, cells_x - 2, rows, lanes],
        lambda c, rows, lanes: x_recv[1, c, rows, lanes],
    )

    for q in range(CHUNKS):
        for side in range(2):
            y_copy(q, side).wait_recv()

        @pl.loop(0, chunk // STEP)
        def _(n):
            for k in range(STEP):
                i = q * chunk + n * STEP + k
                for side, t, mask in ((0, 0, first_row), (1, strips - 1, last_row)):
                    rows = pl.ds(8 * t, 8)
                    for half in range(2):
                        bv = b * tile(1, i, t, half)
                        weight = jnp.where(mask, a - bv if side else a + bv, 0.0)
                        for c in range(comps):
                            before = result[c, i, rows, halves[half]]
                            result[c, i, rows, halves[half]] = before + weight * ghost(side, half, c, i)

    for k in range(1, groups_y):
        sum_copy(k, peer(groups_y - k)).wait_recv()
    for k in range(1, groups_y):
        part_copy(k).wait_send()
        sum_copy(k, tile_y).wait_send()
    for q in range(CHUNKS):
        for side in range(2):
            y_copy(q, side).wait_send()

    @pl.when(tile_x < last_x)
    def _():
        to_east.wait_send()

    @pl.when(tile_x > 0)
    def _():
        to_west.wait_send()


def local(groups_x, groups_y, velocity, inflow, positions, tiles, coefs, counts):
    comps, cells_x, cells_y, depth = velocity.shape
    total_y = cells_y * groups_y
    pos, tiles, coefs = positions[0].transpose(1, 0, 2), tiles[0].T, coefs[0]
    _, recs, points = pos.shape
    velocity, pos, tiles = (
        pltpu.with_memory_space_constraint(x, pltpu.HBM) for x in (velocity, pos, tiles)
    )
    grid = pltpu.VMEM(velocity.shape, F32)
    table = pltpu.VMEM((groups_y, comps, recs * points // (groups_y * LANES), LANES), F32)

    field, _, part, plan, picks, here = pl.pallas_call(
        functools.partial(sample_first, total_y, groups_y),
        out_shape=(
            grid,
            pltpu.VMEM(pos.shape, I32),
            table,
            pltpu.SMEM((8, LANES), I32),
            pltpu.VMEM((recs, depth, points), BF16),
            pltpu.VMEM((recs, points), I32),
        ),
        in_specs=[HBM, HBM, HBM, SMEM],
        out_specs=(VMEM, VMEM, VMEM, SMEM, VMEM, VMEM),
        scratch_shapes=[
            pltpu.VMEM(tiles.shape, I32),
            pltpu.VMEM((8, LANES), I32),
            pltpu.SemaphoreType.DMA((CHUNKS + 3,)),
        ],
        compiler_params=params(),
        name="sample_first",
    )(velocity, pos, tiles, counts)

    def swap(second, *operands):
        sems = 2 * (groups_y - 1) + 2 + 2 * CHUNKS
        return pl.pallas_call(
            functools.partial(exchange, groups_x, groups_y, second),
            out_shape=(grid, table),
            in_specs=[VMEM] * len(operands),
            out_specs=(VMEM, VMEM),
            scratch_shapes=[
                pltpu.VMEM((2, 2, comps, cells_x, LANES), F32),
                pltpu.VMEM((2, 2, comps, cells_x, LANES), F32),
                pltpu.VMEM((2, comps, cells_y, depth), F32),
                pltpu.VMEM((groups_y - 1, *table.shape[1:]), F32),
                pltpu.VMEM(table.shape[1:], F32),
                pltpu.SemaphoreType.DMA((sems,)),
                pltpu.SemaphoreType.DMA((sems,)),
            ],
            compiler_params=params(collective_id=int(second), has_side_effects=True),
            name="exchange_second" if second else "exchange_first",
        )(*operands)

    section, samp_a = swap(False, field, part, inflow)
    section, part = pl.pallas_call(
        spread_and_sample,
        out_shape=(grid, table),
        in_specs=[SMEM] + [VMEM] * 5,
        out_specs=(VMEM, VMEM),
        input_output_aliases={5: 0},
        compiler_params=params(),
        name="spread_and_sample",
    )(plan, picks, here, coefs, samp_a, section)
    final, samp_b = swap(True, field, section, part, inflow)
    _, velocity_next, blade = pl.pallas_call(
        spread_last,
        out_shape=(
            grid,
            jax.ShapeDtypeStruct(velocity.shape, F32),
            jax.ShapeDtypeStruct(pos.shape, F32),
        ),
        in_specs=[SMEM, VMEM, VMEM, VMEM, SMEM, VMEM, VMEM, VMEM],
        out_specs=(VMEM, HBM, HBM),
        input_output_aliases={7: 0},
        scratch_shapes=[pltpu.VMEM(pos.shape, F32), pltpu.SemaphoreType.DMA((CHUNKS + 1,))],
        compiler_params=params(),
        name="spread_last",
    )(plan, picks, here, coefs, counts, samp_a, samp_b, final)
    return (velocity_next, blade.transpose(1, 0, 2)[None])


def solution(mesh):
    return jax.shard_map(
        functools.partial(local, mesh.shape["gx"], mesh.shape["gy"]),
        mesh=mesh,
        in_specs=(
            P(None, "gx", "gy", None),
            P(None, "gy", None),
            P("gx", None, None, None),
            P("gx", None, None),
            P("gx", None, None),
            P("gx"),
        ),
        out_specs=(P(None, "gx", "gy", None), P("gx", None, None, None)),
        check_vma=False,
    )
```

```python
import functools
import math

import jax
import jax.numpy as jnp
from jax import lax
from jax.experimental import pallas as pl
from jax.experimental.pallas import tpu as pltpu
from jax.sharding import PartitionSpec as P

F32, BF16, I32 = jnp.float32, jnp.bfloat16, jnp.int32
RAD = 2
VISCOSITY = 0.05
TIME_STEP = 0.1
WIDTH_EPS = 1.5
K0, K1, K2 = (
    math.exp(-((d / WIDTH_EPS) ** 2)) / (WIDTH_EPS * math.sqrt(math.pi)) for d in range(3)
)
MESH = pl.DeviceIdType.MESH
VMEM = pl.BlockSpec(memory_space=pltpu.VMEM)
SMEM = pl.BlockSpec(memory_space=pltpu.SMEM)
HBM = pl.BlockSpec(memory_space=pltpu.HBM)
LANES = 128
GROUP = 4
STEP = 4
CHUNKS = 4


def params(**kw):
    return pltpu.CompilerParams(vmem_limit_bytes=6 << 20, **kw)


def local_y(pos_y, tile_y, cells_y, total_y):
    return lax.rem(pos_y - tile_y * cells_y + total_y + total_y // 2, total_y) - total_y // 2


def smooth_z(block):
    near = pltpu.roll(block, 1, 1) + pltpu.roll(block, block.shape[1] - 1, 1)
    far = pltpu.roll(block, 2, 1) + pltpu.roll(block, block.shape[1] - 2, 1)
    return K0 * block + K1 * near + K2 * far


def split_dot(block, pick, dims):
    rows = block.shape[0]
    high = block.astype(BF16)
    low = (block - high.astype(F32)).astype(BF16)
    both = lax.dot_general(
        jnp.concatenate([high, low], axis=0), pick, (dims, ((), ())), preferred_element_type=F32
    )
    return both[:rows] + both[rows:]


def build_tables(pos_ref, pick_ref, here_ref, n, rec, tile_y, cells_y, total_y):
    depth, points = pick_ref.shape[1:]
    cell = lax.broadcasted_iota(I32, (depth, points), 0)
    pick_ref[n] = (cell == pos_ref[2, pl.ds(rec, 1), :]).astype(F32).astype(BF16)
    here_ref[pl.ds(n, 1), :] = local_y(pos_ref[1, pl.ds(rec, 1), :], tile_y, cells_y, total_y)


def weight_y(here_ref, n, cells_y):
    here = here_ref[pl.ds(n, 1), :]
    dist = jnp.abs(lax.broadcasted_iota(I32, (cells_y, here.shape[1]), 0) - here)
    return jnp.where(
        dist == 0, K0, jnp.where(dist == 1, K1, jnp.where(dist == 2, K2, 0.0))
    ).astype(F32)


def sample_group(size, field, plan_ref, pick_ref, here_ref, part_ref, group_at, count):
    _, comps, _, cells_y, _ = field.shape
    for k in range(size):
        n = jnp.minimum(size * group_at + k, count - 1)
        rec, hub = plan_ref[0, n], plan_ref[1, n]
        planes = [
            K0 * field[half, :, hub]
            + K1 * (field[half, :, hub - 1] + field[half, :, hub + 1])
            + K2 * (field[half, :, hub - 2] + field[half, :, hub + 2])
            for half in range(2)
        ]
        planes = [value.reshape(comps * cells_y, LANES) for value in planes]
        smooth = smooth_z(jnp.concatenate(planes, axis=1))
        inner = split_dot(smooth, pick_ref[n], ((1,), (0,)))
        value = jnp.sum(inner.reshape(comps, cells_y, -1) * weight_y(here_ref, n, cells_y)[None], axis=1)
        group, row = rec // 8, lax.rem(rec, 8)
        for half in range(2):
            for c in range(comps):
                part_ref[half * 8 + group, c, pl.ds(row, 1), :] = value[
                    c : c + 1, half * LANES : (half + 1) * LANES
                ]


def spread_group(size, field, plan_ref, pick_ref, here_ref, coef_ref, samp_ref, scale, group_at, count):
    _, comps, _, cells_y, _ = field.shape
    slabs = []
    for k in range(size):
        n = jnp.minimum(size * group_at + k, count - 1)
        rec, hub = plan_ref[0, n], plan_ref[1, n]
        factor = jnp.where(size * group_at + k < count, -scale, 0.0)
        group, row = rec // 8, lax.rem(rec, 8)
        sampled = [
            jnp.concatenate(
                [samp_ref[half * 8 + group, c, pl.ds(row, 1), :] for half in range(2)], axis=1
            )
            for c in range(comps)
        ]
        speed = jnp.sqrt(sampled[0] * sampled[0] + sampled[1] * sampled[1] + sampled[2] * sampled[2])
        strength = coef_ref[pl.ds(rec, 1), :] * speed * factor
        along = weight_y(here_ref, n, cells_y)
        weighted = jnp.concatenate([along * (strength * value) for value in sampled], axis=0)
        slab = smooth_z(split_dot(weighted, pick_ref[n], ((1,), (1,))))
        for half in range(2):
            part = slab[:, half * LANES : (half + 1) * LANES]
            slabs.append((half, hub, part.reshape(comps, cells_y, LANES)))
    for half, hub, slab in slabs:
        for d, weight in ((-2, K2), (-1, K1), (0, K0), (1, K1), (2, K2)):
            field[half, :, hub + d] += weight * slab


def make_plan(total_y, groups_y, pos_ref, tiles_ref, counts_ref, rows_ref, cells_x, cells_y):
    recs = pos_ref.shape[1]
    tile_x, tile_y = lax.axis_index("gx"), lax.axis_index("gy")
    rec = lax.broadcasted_iota(I32, (recs, LANES), 0)
    lane = lax.broadcasted_iota(I32, (recs, LANES), 1)
    square = lax.broadcasted_iota(I32, (recs, recs), 0) == lax.broadcasted_iota(I32, (recs, recs), 1)

    def column(row):
        return jnp.sum(jnp.where(square, row.astype(F32), 0.0), axis=1, keepdims=True).astype(I32)

    here = local_y(pos_ref[1], tile_y, cells_y, total_y)
    near = ((here >= -RAD) & (here < cells_y + RAD)).astype(I32)
    touched = jnp.max(near, axis=1, keepdims=True)
    hub = pos_ref[0, :, 0:1] - tile_x * cells_x
    first, number = column(tiles_ref[0:1, :]), column(tiles_ref[1:2, :])
    listed = lax.rem(tile_y - first + groups_y, groups_y) < number
    active = listed & (touched > 0) & (rec[:, 0:1] < counts_ref[0])
    big = jnp.int32(1 << 20)
    key = jnp.where(active, hub * recs + rec[:, 0:1], big)
    key_row = jnp.min(jnp.where(rec == lane, key, big), axis=0, keepdims=True)
    rank = jnp.sum((key_row < key).astype(F32), axis=1, keepdims=True).astype(I32)
    live = active.astype(F32)
    count = jnp.sum(live, axis=0, keepdims=True).astype(I32)
    mine = active & (rank == jnp.minimum(lane, count - 1))
    rows_ref[0:1, :] = jnp.sum(jnp.where(mine, rec, 0).astype(F32), axis=0, keepdims=True).astype(I32)
    rows_ref[1:2, :] = jnp.sum(jnp.where(mine, hub, 0).astype(F32), axis=0, keepdims=True).astype(I32)
    below = active & (hub < lane)
    rows_ref[2:3, :] = jnp.sum(below.astype(F32), axis=0, keepdims=True).astype(I32)


def sample_first(total_y, groups_y, vel_hbm, pos_hbm, tiles_hbm, counts_ref,
                 field, pos_ref, part_ref, plan_ref, pick_ref, here_ref, tiles_ref, rows_ref, sems):
    cells_x, cells_y = field.shape[2:4]
    tile_y = lax.axis_index("gy")
    chunk = cells_x // CHUNKS
    fetch_pos = pltpu.make_async_copy(pos_hbm, pos_ref, sems.at[2 * CHUNKS])
    fetch_tiles = pltpu.make_async_copy(tiles_hbm, tiles_ref, sems.at[2 * CHUNKS + 1])
    fetch_pos.start()
    fetch_tiles.start()
    loads = []
    for q in range(CHUNKS):
        planes = pl.ds(q * chunk, chunk)
        for half in range(2):
            lanes = pl.ds(half * LANES, LANES)
            loads.append(pltpu.make_async_copy(
                vel_hbm.at[:, planes, :, lanes], field.at[half, :, planes], sems.at[2 * q + half]
            ))
            loads[-1].start()
    part_ref[...] = jnp.zeros_like(part_ref)
    rows_ref[...] = jnp.zeros_like(rows_ref)
    fetch_pos.wait()
    fetch_tiles.wait()
    make_plan(total_y, groups_y, pos_ref, tiles_ref, counts_ref, rows_ref, cells_x, cells_y)
    fetch_plan = pltpu.make_async_copy(rows_ref, plan_ref, sems.at[2 * CHUNKS + 2])
    fetch_plan.start()
    fetch_plan.wait()
    count = plan_ref[2, LANES - 1]

    @pl.loop(0, count)
    def _(n):
        build_tables(pos_ref, pick_ref, here_ref, n, plan_ref[0, n], tile_y, cells_y, total_y)

    def sample(size):
        def body(at):
            sample_group(size, field, plan_ref, pick_ref, here_ref, part_ref, at, count)

        return body

    start = jnp.int32(0)
    for q in range(CHUNKS):
        loads[2 * q].wait()
        loads[2 * q + 1].wait()
        stop = (count if q == CHUNKS - 1 else plan_ref[2, (q + 1) * chunk - RAD]) // GROUP
        pl.loop(start, stop)(sample(GROUP))
        start = stop
    pl.loop(start * (GROUP // 2), (count + 1) // 2)(sample(2))


def spread_and_sample(plan_ref, pick_ref, here_ref, coef_ref, samp_ref, _, field, part_ref):
    count = plan_ref[2, LANES - 1]
    part_ref[...] = jnp.zeros_like(part_ref)

    def spread(size):
        def body(at):
            spread_group(size, field, plan_ref, pick_ref, here_ref, coef_ref, samp_ref, TIME_STEP,
                         at, count)

        return body

    def sample(size):
        def body(at):
            sample_group(size, field, plan_ref, pick_ref, here_ref, part_ref, at, count)

        return body

    full = count // GROUP
    for step in (spread, sample):
        pl.loop(0, full)(step(GROUP))
        pl.loop(full * (GROUP // 2), (count + 1) // 2)(step(2))


def spread_last(plan_ref, pick_ref, here_ref, coef_ref, counts_ref, samp_a, samp_b, _,
                field, next_hbm, blade_hbm, blade, sems):
    comps, recs, _ = blade.shape
    chunk = field.shape[2] // CHUNKS
    count = plan_ref[2, LANES - 1]
    for half in range(2):
        lanes = pl.ds(half * LANES, LANES)
        for group in range(recs // 8):
            rows = pl.ds(group * 8, 8)
            a = [samp_a[half * 8 + group, c] for c in range(comps)]
            b = [samp_b[half * 8 + group, c] for c in range(comps)]
            speed_a = jnp.sqrt(a[0] * a[0] + a[1] * a[1] + a[2] * a[2])
            speed_b = jnp.sqrt(b[0] * b[0] + b[1] * b[1] + b[2] * b[2])
            rec = group * 8 + lax.broadcasted_iota(I32, (8, LANES), 0)
            strength = jnp.where(rec < counts_ref[0], coef_ref[rows, lanes] * -0.5, 0.0)
            for c in range(comps):
                blade[c, rows, lanes] = strength * (speed_a * a[c] + speed_b * b[c])
    put = pltpu.make_async_copy(blade, blade_hbm, sems.at[2 * CHUNKS])
    put.start()
    start = jnp.int32(0)
    stores = []
    for q in range(CHUNKS):
        upto = count if q == CHUNKS - 1 else plan_ref[2, (q + 1) * chunk + RAD]
        stop = (upto + GROUP - 1) // GROUP

        @pl.loop(start, stop)
        def _(at):
            spread_group(GROUP, field, plan_ref, pick_ref, here_ref, coef_ref, samp_b,
                         0.5 * TIME_STEP, at, count)

        planes = pl.ds(q * chunk, chunk)
        for half in range(2):
            lanes = pl.ds(half * LANES, LANES)
            stores.append(pltpu.make_async_copy(
                field.at[half, :, planes], next_hbm.at[:, planes, :, lanes], sems.at[2 * q + half]
            ))
            stores[-1].start()
        start = stop

    for store in stores:
        store.wait()
    put.wait()


def exchange(groups_x, groups_y, second, *refs):
    if second:
        old, refs = refs[0], refs[1:]
    (field, part_ref, inflow, result, samp_ref,
     y_send, y_recv, x_recv, gathered, mine, send_sem, recv_sem) = refs
    _, comps, cells_x, cells_y, _ = field.shape
    tile_x, tile_y = lax.axis_index("gx"), lax.axis_index("gy")
    last_x = groups_x - 1

    def peer(k):
        return lax.rem(tile_y + k, groups_y)

    north, south = peer(1), peer(groups_y - 1)
    barrier = pltpu.get_barrier_semaphore()
    for k in range(1, groups_y):
        pl.semaphore_signal(barrier, inc=1, device_id={"gy": peer(k)}, device_id_type=MESH)

    @pl.when(tile_x > 0)
    def _():
        pl.semaphore_signal(barrier, inc=1, device_id={"gx": tile_x - 1}, device_id_type=MESH)

    @pl.when(tile_x < last_x)
    def _():
        pl.semaphore_signal(barrier, inc=1, device_id={"gx": tile_x + 1}, device_id_type=MESH)

    @pl.loop(0, cells_x // 8)
    def _(block):
        rows = pl.ds(block * 8, 8)
        for c in range(comps):
            for half in range(2):
                y_send[0, half, c, rows, :] = field[half, c, rows, 0, :]
                y_send[1, half, c, rows, :] = field[half, c, rows, cells_y - 1, :]

    @pl.when(tile_x == 0)
    def _():
        for half in range(2):
            x_recv[0, half] = inflow[:, :, pl.ds(half * LANES, LANES)]

    @pl.when(tile_x == last_x)
    def _():
        x_recv[1] = field[:, :, cells_x - 1]

    neighbours = (tile_x > 0).astype(I32) + (tile_x < last_x).astype(I32)
    pl.semaphore_wait(barrier, groups_y - 1 + neighbours)

    def remote(src, dst, slot, where):
        return pltpu.make_async_remote_copy(
            src_ref=src, dst_ref=dst, send_sem=send_sem.at[slot], recv_sem=recv_sem.at[slot],
            device_id=where, device_id_type=MESH,
        )

    def part_copy(k):
        return remote(part_ref.at[peer(k)], gathered.at[k - 1], 0, {"gy": peer(k)})

    def sum_copy(k, owner):
        return remote(mine, samp_ref.at[owner], 1, {"gy": peer(k)})

    def every(sem):
        return pltpu.make_async_copy(gathered, gathered, sem)

    base = 1
    chunk = cells_x // CHUNKS

    def y_copy(q, side):
        rows = pl.ds(q * chunk, chunk)
        return remote(y_send.at[1 - side, :, :, rows, :], y_recv.at[side, :, :, rows, :],
                      2 * base + 2 + 2 * q + side, {"gy": south if side else north})

    to_east = remote(field.at[:, :, cells_x - 1], x_recv.at[0], 2 * base, {"gx": tile_x + 1})
    to_west = remote(field.at[:, :, 0], x_recv.at[1], 2 * base + 1, {"gx": tile_x - 1})

    for k in range(1, groups_y):
        part_copy(k).start()
    for q in range(CHUNKS):
        for side in range(2):
            y_copy(q, side).start()

    @pl.when(tile_x < last_x)
    def _():
        to_east.start()

    @pl.when(tile_x > 0)
    def _():
        to_west.start()

    scale = 0.5 if second else 1.0
    a = scale * TIME_STEP * VISCOSITY
    b = scale * TIME_STEP * 0.5
    centre = scale * (1.0 - 6.0 * TIME_STEP * VISCOSITY)
    sub = lax.broadcasted_iota(I32, (8, LANES), 0)
    lane = lax.broadcasted_iota(I32, (8, LANES), 1)
    first_row, last_row = sub == 0, sub == 7
    first_lane, last_lane = lane == 0, lane == LANES - 1
    zero = jnp.zeros((8, LANES), F32)
    strips = cells_y // 8

    def tile(c, i, t, half):
        return field[half, c, i, pl.ds(8 * t, 8), :]

    def ghost(side, half, c, i):
        return y_recv[side, half, c, pl.ds(i, 8, stride=0), :]

    def plane(i, west, east):
        for t in range(strips):
            rows = pl.ds(8 * t, 8)
            here = [[tile(c, i, t, half) for half in range(2)] for c in range(comps)]
            lower, upper = [], []
            for c in range(comps):
                up = [pltpu.roll(v, 1, 1) for v in here[c]]
                down = [pltpu.roll(v, LANES - 1, 1) for v in here[c]]
                lower.append([jnp.where(first_lane, zero, up[0]), jnp.where(first_lane, up[0], up[1])])
                upper.append([jnp.where(last_lane, down[1], down[0]), jnp.where(last_lane, zero, down[1])])
            for half in range(2):
                bu, bv, bw = (b * here[c][half] for c in range(3))
                for c in range(comps):
                    value = here[c][half]
                    if t > 0:
                        to_s = field[half, c, i, pl.ds(8 * t - 1, 8), :]
                    else:
                        to_s = jnp.where(first_row, zero, pltpu.roll(value, 1, 0))
                    if t < strips - 1:
                        to_n = field[half, c, i, pl.ds(8 * t + 1, 8), :]
                    else:
                        to_n = jnp.where(last_row, zero, pltpu.roll(value, 7, 0))
                    out = (
                        centre * value
                        + ((a - bu) * east(half, c, rows) + (a + bu) * west(half, c, rows))
                        + ((a - bv) * to_n + (a + bv) * to_s)
                        + ((a - bw) * upper[c][half] + (a + bw) * lower[c][half])
                    )
                    if second:
                        out = out + 0.5 * old[half, c, i, rows, :]
                    result[half, c, i, rows, :] = out

    def inside(i):
        plane(
            i,
            lambda half, c, rows: field[half, c, i - 1, rows, :],
            lambda half, c, rows: field[half, c, i + 1, rows, :],
        )

    def piece(start, stop):
        @pl.loop(0, (stop - start) // STEP)
        def _(n):
            for k in range(STEP):
                inside(start + n * STEP + k)

    steps = (cells_x - 2) // STEP
    cuts = [1 + STEP * (steps * k // 4) for k in (0, 2, 4)]

    piece(cuts[0], cuts[1])
    every(recv_sem.at[0]).wait()
    total = functools.reduce(jnp.add, [gathered[k] for k in range(groups_y - 1)], part_ref[tile_y])
    mine[...] = total
    samp_ref[tile_y] = total
    for k in range(1, groups_y):
        sum_copy(k, tile_y).start()
    piece(cuts[1], cuts[2])
    for i in range(cuts[2], cells_x - 1):
        inside(i)

    @pl.when(tile_x > 0)
    def _():
        to_east.wait_recv()

    @pl.when(tile_x < last_x)
    def _():
        to_west.wait_recv()

    plane(
        0,
        lambda half, c, rows: x_recv[0, half, c, rows, :],
        lambda half, c, rows: field[half, c, 1, rows, :],
    )
    plane(
        cells_x - 1,
        lambda half, c, rows: field[half, c, cells_x - 2, rows, :],
        lambda half, c, rows: x_recv[1, half, c, rows, :],
    )

    for q in range(CHUNKS):
        for side in range(2):
            y_copy(q, side).wait_recv()

        @pl.loop(0, chunk // STEP)
        def _(n):
            for k in range(STEP):
                i = q * chunk + n * STEP + k
                for side, t, mask in ((0, 0, first_row), (1, strips - 1, last_row)):
                    rows = pl.ds(8 * t, 8)
                    for half in range(2):
                        bv = b * tile(1, i, t, half)
                        weight = jnp.where(mask, a - bv if side else a + bv, 0.0)
                        for c in range(comps):
                            before = result[half, c, i, rows, :]
                            result[half, c, i, rows, :] = before + weight * ghost(side, half, c, i)

    every(recv_sem.at[1]).wait()
    every(send_sem.at[0]).wait()
    every(send_sem.at[1]).wait()
    for q in range(CHUNKS):
        for side in range(2):
            y_copy(q, side).wait_send()

    @pl.when(tile_x < last_x)
    def _():
        to_east.wait_send()

    @pl.when(tile_x > 0)
    def _():
        to_west.wait_send()


def local(groups_x, groups_y, velocity, inflow, positions, tiles, coefs, counts):
    comps, cells_x, cells_y, depth = velocity.shape
    total_y = cells_y * groups_y
    pos, tiles, coefs = positions[0].transpose(1, 0, 2), tiles[0].T, coefs[0]
    _, recs, points = pos.shape
    velocity, pos, tiles = (
        pltpu.with_memory_space_constraint(x, pltpu.HBM) for x in (velocity, pos, tiles)
    )
    grid = pltpu.VMEM((2, comps, cells_x, cells_y, LANES), F32)
    table = pltpu.VMEM((groups_y, comps, recs * points // (groups_y * LANES), LANES), F32)

    field, _, part, plan, picks, here = pl.pallas_call(
        functools.partial(sample_first, total_y, groups_y),
        out_shape=(
            grid,
            pltpu.VMEM(pos.shape, I32),
            table,
            pltpu.SMEM((8, LANES), I32),
            pltpu.VMEM((recs, depth, points), BF16),
            pltpu.VMEM((recs, points), I32),
        ),
        in_specs=[HBM, HBM, HBM, SMEM],
        out_specs=(VMEM, VMEM, VMEM, SMEM, VMEM, VMEM),
        scratch_shapes=[
            pltpu.VMEM(tiles.shape, I32),
            pltpu.VMEM((8, LANES), I32),
            pltpu.SemaphoreType.DMA((2 * CHUNKS + 3,)),
        ],
        compiler_params=params(),
        name="sample_first",
    )(velocity, pos, tiles, counts)

    def swap(second, *operands):
        sems = 4 + 2 * CHUNKS
        return pl.pallas_call(
            functools.partial(exchange, groups_x, groups_y, second),
            out_shape=(grid, table),
            in_specs=[VMEM] * len(operands),
            out_specs=(VMEM, VMEM),
            scratch_shapes=[
                pltpu.VMEM((2, 2, comps, cells_x, LANES), F32),
                pltpu.VMEM((2, 2, comps, cells_x, LANES), F32),
                pltpu.VMEM((2, 2, comps, cells_y, LANES), F32),
                pltpu.VMEM((groups_y - 1, *table.shape[1:]), F32),
                pltpu.VMEM(table.shape[1:], F32),
                pltpu.SemaphoreType.DMA((sems,)),
                pltpu.SemaphoreType.DMA((sems,)),
            ],
            compiler_params=params(collective_id=int(second), has_side_effects=True),
            name="exchange_second" if second else "exchange_first",
        )(*operands)

    section, samp_a = swap(False, field, part, inflow)
    section, part = pl.pallas_call(
        spread_and_sample,
        out_shape=(grid, table),
        in_specs=[SMEM] + [VMEM] * 5,
        out_specs=(VMEM, VMEM),
        input_output_aliases={5: 0},
        compiler_params=params(),
        name="spread_and_sample",
    )(plan, picks, here, coefs, samp_a, section)
    final, samp_b = swap(True, field, section, part, inflow)
    _, velocity_next, blade = pl.pallas_call(
        spread_last,
        out_shape=(
            grid,
            jax.ShapeDtypeStruct(velocity.shape, F32),
            jax.ShapeDtypeStruct(pos.shape, F32),
        ),
        in_specs=[SMEM, VMEM, VMEM, VMEM, SMEM, VMEM, VMEM, VMEM],
        out_specs=(VMEM, HBM, HBM),
        input_output_aliases={7: 0},
        scratch_shapes=[pltpu.VMEM(pos.shape, F32), pltpu.SemaphoreType.DMA((2 * CHUNKS + 1,))],
        compiler_params=params(),
        name="spread_last",
    )(plan, picks, here, coefs, counts, samp_a, samp_b, final)
    return (velocity_next, blade.transpose(1, 0, 2)[None])


def solution(mesh):
    return jax.shard_map(
        functools.partial(local, mesh.shape["gx"], mesh.shape["gy"]),
        mesh=mesh,
        in_specs=(
            P(None, "gx", "gy", None),
            P(None, "gy", None),
            P("gx", None, None, None),
            P("gx", None, None),
            P("gx", None, None),
            P("gx"),
        ),
        out_specs=(P(None, "gx", "gy", None), P("gx", None, None, None)),
        check_vma=False,
    )
```

```python
import functools
import math

import jax
import jax.numpy as jnp
from jax import lax
from jax.experimental import pallas as pl
from jax.experimental.pallas import tpu as pltpu
from jax.sharding import PartitionSpec as P

F32, BF16, I32 = jnp.float32, jnp.bfloat16, jnp.int32
RAD = 2
VISCOSITY = 0.05
TIME_STEP = 0.1
WIDTH_EPS = 1.5
K0, K1, K2 = (
    math.exp(-((d / WIDTH_EPS) ** 2)) / (WIDTH_EPS * math.sqrt(math.pi)) for d in range(3)
)
MESH = pl.DeviceIdType.MESH
VMEM = pl.BlockSpec(memory_space=pltpu.VMEM)
SMEM = pl.BlockSpec(memory_space=pltpu.SMEM)
HBM = pl.BlockSpec(memory_space=pltpu.HBM)
LANES = 128
GROUP, SMALL = 8, 4
STEP = 4
CHUNKS = 4


def params(**kw):
    return pltpu.CompilerParams(vmem_limit_bytes=6 << 20, **kw)


def local_y(pos_y, tile_y, cells_y, total_y):
    return lax.rem(pos_y - tile_y * cells_y + total_y + total_y // 2, total_y) - total_y // 2


def smooth_z(block):
    near = pltpu.roll(block, 1, 1) + pltpu.roll(block, block.shape[1] - 1, 1)
    far = pltpu.roll(block, 2, 1) + pltpu.roll(block, block.shape[1] - 2, 1)
    return K0 * block + K1 * near + K2 * far


def split_dot(block, pick, dims):
    rows = block.shape[0]
    high = block.astype(BF16)
    low = (block - high.astype(F32)).astype(BF16)
    both = lax.dot_general(
        jnp.concatenate([high, low], axis=0), pick, (dims, ((), ())), preferred_element_type=F32
    )
    return both[:rows] + both[rows:]


def build_tables(pos_ref, pick_ref, here_ref, n, rec, tile_y, cells_y, total_y):
    depth, points = pick_ref.shape[1:]
    cell = lax.broadcasted_iota(I32, (depth, points), 0)
    pick_ref[n] = (cell == pos_ref[2, pl.ds(rec, 1), :]).astype(F32).astype(BF16)
    here_ref[pl.ds(n, 1), :] = local_y(pos_ref[1, pl.ds(rec, 1), :], tile_y, cells_y, total_y)


def weight_y(here_ref, n, cells_y):
    here = here_ref[pl.ds(n, 1), :]
    dist = jnp.abs(lax.broadcasted_iota(I32, (cells_y, here.shape[1]), 0) - here)
    return jnp.where(
        dist == 0, K0, jnp.where(dist == 1, K1, jnp.where(dist == 2, K2, 0.0))
    ).astype(F32)


def sample_group(size, field, plan_ref, pick_ref, here_ref, part_ref, group_at, count):
    _, comps, _, cells_y, _ = field.shape
    for k in range(size):
        n = jnp.minimum(size * group_at + k, count - 1)
        rec, hub = plan_ref[0, n], plan_ref[1, n]
        planes = [
            K0 * field[half, :, hub]
            + K1 * (field[half, :, hub - 1] + field[half, :, hub + 1])
            + K2 * (field[half, :, hub - 2] + field[half, :, hub + 2])
            for half in range(2)
        ]
        planes = [value.reshape(comps * cells_y, LANES) for value in planes]
        smooth = smooth_z(jnp.concatenate(planes, axis=1))
        inner = split_dot(smooth, pick_ref[n], ((1,), (0,)))
        value = jnp.sum(inner.reshape(comps, cells_y, -1) * weight_y(here_ref, n, cells_y)[None], axis=1)
        group, row = rec // 8, lax.rem(rec, 8)
        for half in range(2):
            for c in range(comps):
                part_ref[half * 8 + group, c, pl.ds(row, 1), :] = value[
                    c : c + 1, half * LANES : (half + 1) * LANES
                ]


def spread_group(size, field, plan_ref, pick_ref, here_ref, coef_ref, samp_ref, scale, group_at, count):
    _, comps, _, cells_y, _ = field.shape
    slabs = []
    for k in range(size):
        n = jnp.minimum(size * group_at + k, count - 1)
        rec, hub = plan_ref[0, n], plan_ref[1, n]
        factor = jnp.where(size * group_at + k < count, -scale, 0.0)
        group, row = rec // 8, lax.rem(rec, 8)
        sampled = [
            jnp.concatenate(
                [samp_ref[half * 8 + group, c, pl.ds(row, 1), :] for half in range(2)], axis=1
            )
            for c in range(comps)
        ]
        speed = jnp.sqrt(sampled[0] * sampled[0] + sampled[1] * sampled[1] + sampled[2] * sampled[2])
        strength = coef_ref[pl.ds(rec, 1), :] * speed * factor
        along = weight_y(here_ref, n, cells_y)
        weighted = jnp.concatenate([along * (strength * value) for value in sampled], axis=0)
        slab = smooth_z(split_dot(weighted, pick_ref[n], ((1,), (1,))))
        for half in range(2):
            part = slab[:, half * LANES : (half + 1) * LANES]
            slabs.append((half, hub, part.reshape(comps, cells_y, LANES)))
    for half, hub, slab in slabs:
        for d, weight in ((-2, K2), (-1, K1), (0, K0), (1, K1), (2, K2)):
            field[half, :, hub + d] += weight * slab


def make_plan(total_y, groups_y, pos_ref, tiles_ref, counts_ref, rows_ref, cells_x, cells_y):
    recs = pos_ref.shape[1]
    tile_x, tile_y = lax.axis_index("gx"), lax.axis_index("gy")
    rec = lax.broadcasted_iota(I32, (recs, LANES), 0)
    lane = lax.broadcasted_iota(I32, (recs, LANES), 1)
    square = lax.broadcasted_iota(I32, (recs, recs), 0) == lax.broadcasted_iota(I32, (recs, recs), 1)

    def column(row):
        return jnp.sum(jnp.where(square, row.astype(F32), 0.0), axis=1, keepdims=True).astype(I32)

    here = local_y(pos_ref[1], tile_y, cells_y, total_y)
    near = ((here >= -RAD) & (here < cells_y + RAD)).astype(I32)
    touched = jnp.max(near, axis=1, keepdims=True)
    hub = pos_ref[0, :, 0:1] - tile_x * cells_x
    first, number = column(tiles_ref[0:1, :]), column(tiles_ref[1:2, :])
    listed = lax.rem(tile_y - first + groups_y, groups_y) < number
    active = listed & (touched > 0) & (rec[:, 0:1] < counts_ref[0])
    big = jnp.int32(1 << 20)
    key = jnp.where(active, hub * recs + rec[:, 0:1], big)
    key_row = jnp.min(jnp.where(rec == lane, key, big), axis=0, keepdims=True)
    rank = jnp.sum((key_row < key).astype(F32), axis=1, keepdims=True).astype(I32)
    live = active.astype(F32)
    count = jnp.sum(live, axis=0, keepdims=True).astype(I32)
    mine = active & (rank == jnp.minimum(lane, count - 1))
    rows_ref[0:1, :] = jnp.sum(jnp.where(mine, rec, 0).astype(F32), axis=0, keepdims=True).astype(I32)
    rows_ref[1:2, :] = jnp.sum(jnp.where(mine, hub, 0).astype(F32), axis=0, keepdims=True).astype(I32)
    below = active & (hub < lane)
    rows_ref[2:3, :] = jnp.sum(below.astype(F32), axis=0, keepdims=True).astype(I32)


def over_records(count, step):
    full = count // GROUP
    pl.loop(0, full)(step(GROUP))
    pl.loop(full * (GROUP // SMALL), (count + SMALL - 1) // SMALL)(step(SMALL))


def sample_first(total_y, groups_y, vel_hbm, pos_hbm, tiles_hbm, counts_ref,
                 field, pos_ref, part_ref, plan_ref, pick_ref, here_ref, tiles_ref, rows_ref, sems):
    cells_x, cells_y = field.shape[2:4]
    tile_y = lax.axis_index("gy")
    chunk = cells_x // CHUNKS
    fetch_pos = pltpu.make_async_copy(pos_hbm, pos_ref, sems.at[2 * CHUNKS])
    fetch_tiles = pltpu.make_async_copy(tiles_hbm, tiles_ref, sems.at[2 * CHUNKS + 1])
    fetch_pos.start()
    fetch_tiles.start()
    loads = []
    for q in range(CHUNKS):
        planes = pl.ds(q * chunk, chunk)
        for half in range(2):
            lanes = pl.ds(half * LANES, LANES)
            loads.append(pltpu.make_async_copy(
                vel_hbm.at[:, planes, :, lanes], field.at[half, :, planes], sems.at[2 * q + half]
            ))
            loads[-1].start()
    part_ref[...] = jnp.zeros_like(part_ref)
    rows_ref[...] = jnp.zeros_like(rows_ref)
    fetch_pos.wait()
    fetch_tiles.wait()
    make_plan(total_y, groups_y, pos_ref, tiles_ref, counts_ref, rows_ref, cells_x, cells_y)
    fetch_plan = pltpu.make_async_copy(rows_ref, plan_ref, sems.at[2 * CHUNKS + 2])
    fetch_plan.start()
    fetch_plan.wait()
    count = plan_ref[2, LANES - 1]

    @pl.loop(0, count)
    def _(n):
        build_tables(pos_ref, pick_ref, here_ref, n, plan_ref[0, n], tile_y, cells_y, total_y)

    def sample(size):
        def body(at):
            sample_group(size, field, plan_ref, pick_ref, here_ref, part_ref, at, count)

        return body

    for load in loads:
        load.wait()
    over_records(count, sample)


def spread_and_sample(plan_ref, pick_ref, here_ref, coef_ref, samp_ref, _, field, part_ref):
    count = plan_ref[2, LANES - 1]
    part_ref[...] = jnp.zeros_like(part_ref)

    def spread(size):
        def body(at):
            spread_group(size, field, plan_ref, pick_ref, here_ref, coef_ref, samp_ref, TIME_STEP,
                         at, count)

        return body

    def sample(size):
        def body(at):
            sample_group(size, field, plan_ref, pick_ref, here_ref, part_ref, at, count)

        return body

    over_records(count, spread)
    over_records(count, sample)


def spread_last(plan_ref, pick_ref, here_ref, coef_ref, counts_ref, samp_a, samp_b, _,
                field, next_hbm, blade_hbm, blade, sems):
    comps, recs, _ = blade.shape
    chunk = field.shape[2] // CHUNKS
    count = plan_ref[2, LANES - 1]
    for half in range(2):
        lanes = pl.ds(half * LANES, LANES)
        for group in range(recs // 8):
            rows = pl.ds(group * 8, 8)
            a = [samp_a[half * 8 + group, c] for c in range(comps)]
            b = [samp_b[half * 8 + group, c] for c in range(comps)]
            speed_a = jnp.sqrt(a[0] * a[0] + a[1] * a[1] + a[2] * a[2])
            speed_b = jnp.sqrt(b[0] * b[0] + b[1] * b[1] + b[2] * b[2])
            rec = group * 8 + lax.broadcasted_iota(I32, (8, LANES), 0)
            strength = jnp.where(rec < counts_ref[0], coef_ref[rows, lanes] * -0.5, 0.0)
            for c in range(comps):
                blade[c, rows, lanes] = strength * (speed_a * a[c] + speed_b * b[c])
    put = pltpu.make_async_copy(blade, blade_hbm, sems.at[2 * CHUNKS])
    put.start()
    full = count // GROUP

    def spread(size):
        def body(at):
            spread_group(size, field, plan_ref, pick_ref, here_ref, coef_ref, samp_b,
                         0.5 * TIME_STEP, at, count)

        return body

    def store(q, half):
        planes, lanes = pl.ds(q * chunk, chunk), pl.ds(half * LANES, LANES)
        return pltpu.make_async_copy(
            field.at[half, :, planes], next_hbm.at[:, planes, :, lanes], sems.at[2 * q + half]
        )

    def finish(q, done):
        large, small = done
        upto = jnp.where(q == CHUNKS - 1, count, plan_ref[2, (q + 1) * chunk + RAD])
        large_stop = jnp.minimum((upto + GROUP - 1) // GROUP, full)
        small_stop = jnp.maximum((upto + SMALL - 1) // SMALL, small)
        pl.loop(large, large_stop)(spread(GROUP))
        pl.loop(small, small_stop)(spread(SMALL))
        for half in range(2):
            store(q, half).start()
        return large_stop, small_stop

    lax.fori_loop(0, CHUNKS, finish, (jnp.int32(0), full * (GROUP // SMALL)))
    for q in range(CHUNKS):
        for half in range(2):
            store(q, half).wait()
    put.wait()


def exchange(groups_x, groups_y, second, *refs):
    if second:
        old, refs = refs[0], refs[1:]
    (field, part_ref, inflow, result, samp_ref,
     y_send, y_recv, x_recv, gathered, mine, send_sem, recv_sem) = refs
    _, comps, cells_x, cells_y, _ = field.shape
    tile_x, tile_y = lax.axis_index("gx"), lax.axis_index("gy")
    last_x = groups_x - 1

    def peer(k):
        return lax.rem(tile_y + k, groups_y)

    north, south = peer(1), peer(groups_y - 1)
    barrier = pltpu.get_barrier_semaphore()
    for k in range(1, groups_y):
        pl.semaphore_signal(barrier, inc=1, device_id={"gy": peer(k)}, device_id_type=MESH)

    @pl.when(tile_x > 0)
    def _():
        pl.semaphore_signal(barrier, inc=1, device_id={"gx": tile_x - 1}, device_id_type=MESH)

    @pl.when(tile_x < last_x)
    def _():
        pl.semaphore_signal(barrier, inc=1, device_id={"gx": tile_x + 1}, device_id_type=MESH)

    @pl.loop(0, cells_x // 8)
    def _(block):
        rows = pl.ds(block * 8, 8)
        for c in range(comps):
            for half in range(2):
                y_send[0, half, c, rows, :] = field[half, c, rows, 0, :]
                y_send[1, half, c, rows, :] = field[half, c, rows, cells_y - 1, :]

    @pl.when(tile_x == 0)
    def _():
        for half in range(2):
            x_recv[0, half] = inflow[:, :, pl.ds(half * LANES, LANES)]

    @pl.when(tile_x == last_x)
    def _():
        x_recv[1] = field[:, :, cells_x - 1]

    neighbours = (tile_x > 0).astype(I32) + (tile_x < last_x).astype(I32)
    pl.semaphore_wait(barrier, groups_y - 1 + neighbours)

    def remote(src, dst, slot, where):
        return pltpu.make_async_remote_copy(
            src_ref=src, dst_ref=dst, send_sem=send_sem.at[slot], recv_sem=recv_sem.at[slot],
            device_id=where, device_id_type=MESH,
        )

    def part_copy(k):
        return remote(part_ref.at[peer(k)], gathered.at[k - 1], 0, {"gy": peer(k)})

    def sum_copy(k, owner):
        return remote(mine, samp_ref.at[owner], 1, {"gy": peer(k)})

    def every(sem):
        return pltpu.make_async_copy(gathered, gathered, sem)

    base = 1
    chunk = cells_x // CHUNKS

    def y_copy(q, side):
        rows = pl.ds(q * chunk, chunk)
        return remote(y_send.at[1 - side, :, :, rows, :], y_recv.at[side, :, :, rows, :],
                      2 * base + 2 + 2 * q + side, {"gy": south if side else north})

    to_east = remote(field.at[:, :, cells_x - 1], x_recv.at[0], 2 * base, {"gx": tile_x + 1})
    to_west = remote(field.at[:, :, 0], x_recv.at[1], 2 * base + 1, {"gx": tile_x - 1})

    for k in range(1, groups_y):
        part_copy(k).start()
    for q in range(CHUNKS - 1):
        for side in range(2):
            y_copy(q, side).start()

    @pl.when(tile_x < last_x)
    def _():
        to_east.start()

    @pl.when(tile_x > 0)
    def _():
        to_west.start()

    scale = 0.5 if second else 1.0
    a = scale * TIME_STEP * VISCOSITY
    b = scale * TIME_STEP * 0.5
    centre = scale * (1.0 - 6.0 * TIME_STEP * VISCOSITY)
    sub = lax.broadcasted_iota(I32, (8, LANES), 0)
    lane = lax.broadcasted_iota(I32, (8, LANES), 1)
    first_row, last_row = sub == 0, sub == 7
    first_lane, last_lane = lane == 0, lane == LANES - 1
    zero = jnp.zeros((8, LANES), F32)
    strips = cells_y // 8

    def tile(c, i, t, half):
        return field[half, c, i, pl.ds(8 * t, 8), :]

    def ghost(side, half, c, i):
        return y_recv[side, half, c, pl.ds(i, 8, stride=0), :]

    def plane(i, west, east):
        for t in range(strips):
            rows = pl.ds(8 * t, 8)
            here = [[tile(c, i, t, half) for half in range(2)] for c in range(comps)]
            lower, upper = [], []
            for c in range(comps):
                up = [pltpu.roll(v, 1, 1) for v in here[c]]
                down = [pltpu.roll(v, LANES - 1, 1) for v in here[c]]
                lower.append([jnp.where(first_lane, zero, up[0]), jnp.where(first_lane, up[0], up[1])])
                upper.append([jnp.where(last_lane, down[1], down[0]), jnp.where(last_lane, zero, down[1])])
            for half in range(2):
                bu, bv, bw = (b * here[c][half] for c in range(3))
                for c in range(comps):
                    value = here[c][half]
                    if t > 0:
                        to_s = field[half, c, i, pl.ds(8 * t - 1, 8), :]
                    else:
                        to_s = jnp.where(first_row, zero, pltpu.roll(value, 1, 0))
                    if t < strips - 1:
                        to_n = field[half, c, i, pl.ds(8 * t + 1, 8), :]
                    else:
                        to_n = jnp.where(last_row, zero, pltpu.roll(value, 7, 0))
                    out = (
                        centre * value
                        + ((a - bu) * east(half, c, rows) + (a + bu) * west(half, c, rows))
                        + ((a - bv) * to_n + (a + bv) * to_s)
                        + ((a - bw) * upper[c][half] + (a + bw) * lower[c][half])
                    )
                    if second:
                        out = out + 0.5 * old[half, c, i, rows, :]
                    result[half, c, i, rows, :] = out

    def inside(i):
        plane(
            i,
            lambda half, c, rows: field[half, c, i - 1, rows, :],
            lambda half, c, rows: field[half, c, i + 1, rows, :],
        )

    def piece(start, stop):
        @pl.loop(0, (stop - start) // STEP)
        def _(n):
            for k in range(STEP):
                inside(start + n * STEP + k)

    steps = (cells_x - 2) // STEP
    cuts = [1 + STEP * (steps * k // 4) for k in (0, 2, 4)]

    piece(cuts[0], cuts[1])
    every(recv_sem.at[0]).wait()
    total = functools.reduce(jnp.add, [gathered[k] for k in range(groups_y - 1)], part_ref[tile_y])
    mine[...] = total
    samp_ref[tile_y] = total
    for k in range(1, groups_y):
        sum_copy(k, tile_y).start()
    for q in (CHUNKS - 1,):
        for side in range(2):
            y_copy(q, side).start()
    piece(cuts[1], cuts[2])
    for i in range(cuts[2], cells_x - 1):
        inside(i)

    @pl.when(tile_x > 0)
    def _():
        to_east.wait_recv()

    @pl.when(tile_x < last_x)
    def _():
        to_west.wait_recv()

    plane(
        0,
        lambda half, c, rows: x_recv[0, half, c, rows, :],
        lambda half, c, rows: field[half, c, 1, rows, :],
    )
    plane(
        cells_x - 1,
        lambda half, c, rows: field[half, c, cells_x - 2, rows, :],
        lambda half, c, rows: x_recv[1, half, c, rows, :],
    )

    for q in range(CHUNKS):
        for side in range(2):
            y_copy(q, side).wait_recv()

        @pl.loop(0, chunk // STEP)
        def _(n):
            for k in range(STEP):
                i = q * chunk + n * STEP + k
                for side, t, mask in ((0, 0, first_row), (1, strips - 1, last_row)):
                    rows = pl.ds(8 * t, 8)
                    for half in range(2):
                        bv = b * tile(1, i, t, half)
                        weight = jnp.where(mask, a - bv if side else a + bv, 0.0)
                        for c in range(comps):
                            before = result[half, c, i, rows, :]
                            result[half, c, i, rows, :] = before + weight * ghost(side, half, c, i)

    every(recv_sem.at[1]).wait()
    every(send_sem.at[0]).wait()
    every(send_sem.at[1]).wait()
    for q in range(CHUNKS):
        for side in range(2):
            y_copy(q, side).wait_send()

    @pl.when(tile_x < last_x)
    def _():
        to_east.wait_send()

    @pl.when(tile_x > 0)
    def _():
        to_west.wait_send()


def local(groups_x, groups_y, velocity, inflow, positions, tiles, coefs, counts):
    comps, cells_x, cells_y, depth = velocity.shape
    total_y = cells_y * groups_y
    pos, tiles, coefs = positions[0].transpose(1, 0, 2), tiles[0].T, coefs[0]
    _, recs, points = pos.shape
    velocity, pos, tiles = (
        pltpu.with_memory_space_constraint(x, pltpu.HBM) for x in (velocity, pos, tiles)
    )
    grid = pltpu.VMEM((2, comps, cells_x, cells_y, LANES), F32)
    table = pltpu.VMEM((groups_y, comps, recs * points // (groups_y * LANES), LANES), F32)

    field, _, part, plan, picks, here = pl.pallas_call(
        functools.partial(sample_first, total_y, groups_y),
        out_shape=(
            grid,
            pltpu.VMEM(pos.shape, I32),
            table,
            pltpu.SMEM((8, LANES), I32),
            pltpu.VMEM((recs, depth, points), BF16),
            pltpu.VMEM((recs, points), I32),
        ),
        in_specs=[HBM, HBM, HBM, SMEM],
        out_specs=(VMEM, VMEM, VMEM, SMEM, VMEM, VMEM),
        scratch_shapes=[
            pltpu.VMEM(tiles.shape, I32),
            pltpu.VMEM((8, LANES), I32),
            pltpu.SemaphoreType.DMA((2 * CHUNKS + 3,)),
        ],
        compiler_params=params(),
        name="sample_first",
    )(velocity, pos, tiles, counts)

    def swap(second, *operands):
        sems = 4 + 2 * CHUNKS
        return pl.pallas_call(
            functools.partial(exchange, groups_x, groups_y, second),
            out_shape=(grid, table),
            in_specs=[VMEM] * len(operands),
            out_specs=(VMEM, VMEM),
            scratch_shapes=[
                pltpu.VMEM((2, 2, comps, cells_x, LANES), F32),
                pltpu.VMEM((2, 2, comps, cells_x, LANES), F32),
                pltpu.VMEM((2, 2, comps, cells_y, LANES), F32),
                pltpu.VMEM((groups_y - 1, *table.shape[1:]), F32),
                pltpu.VMEM(table.shape[1:], F32),
                pltpu.SemaphoreType.DMA((sems,)),
                pltpu.SemaphoreType.DMA((sems,)),
            ],
            compiler_params=params(collective_id=int(second), has_side_effects=True),
            name="exchange_second" if second else "exchange_first",
        )(*operands)

    section, samp_a = swap(False, field, part, inflow)
    section, part = pl.pallas_call(
        spread_and_sample,
        out_shape=(grid, table),
        in_specs=[SMEM] + [VMEM] * 5,
        out_specs=(VMEM, VMEM),
        input_output_aliases={5: 0},
        compiler_params=params(),
        name="spread_and_sample",
    )(plan, picks, here, coefs, samp_a, section)
    final, samp_b = swap(True, field, section, part, inflow)
    _, velocity_next, blade = pl.pallas_call(
        spread_last,
        out_shape=(
            grid,
            jax.ShapeDtypeStruct(velocity.shape, F32),
            jax.ShapeDtypeStruct(pos.shape, F32),
        ),
        in_specs=[SMEM, VMEM, VMEM, VMEM, SMEM, VMEM, VMEM, VMEM],
        out_specs=(VMEM, HBM, HBM),
        input_output_aliases={7: 0},
        scratch_shapes=[pltpu.VMEM(pos.shape, F32), pltpu.SemaphoreType.DMA((2 * CHUNKS + 1,))],
        compiler_params=params(),
        name="spread_last",
    )(plan, picks, here, coefs, counts, samp_a, samp_b, final)
    return (velocity_next, blade.transpose(1, 0, 2)[None])


def solution(mesh):
    return jax.shard_map(
        functools.partial(local, mesh.shape["gx"], mesh.shape["gy"]),
        mesh=mesh,
        in_specs=(
            P(None, "gx", "gy", None),
            P(None, "gy", None),
            P("gx", None, None, None),
            P("gx", None, None),
            P("gx", None, None),
            P("gx"),
        ),
        out_specs=(P(None, "gx", "gy", None), P("gx", None, None, None)),
        check_vma=False,
    )
```

```python
import functools
import math

import jax
import jax.numpy as jnp
from jax import lax
from jax.experimental import pallas as pl
from jax.experimental.pallas import tpu as pltpu
from jax.sharding import PartitionSpec as P

F32, BF16, I32 = jnp.float32, jnp.bfloat16, jnp.int32
RAD = 2
VISCOSITY = 0.05
TIME_STEP = 0.1
WIDTH_EPS = 1.5
K0, K1, K2 = (
    math.exp(-((d / WIDTH_EPS) ** 2)) / (WIDTH_EPS * math.sqrt(math.pi)) for d in range(3)
)
MESH = pl.DeviceIdType.MESH
VMEM = pl.BlockSpec(memory_space=pltpu.VMEM)
SMEM = pl.BlockSpec(memory_space=pltpu.SMEM)
HBM = pl.BlockSpec(memory_space=pltpu.HBM)
LANES = 128
GROUP, SMALL = 8, 4
STEP = 4
CHUNKS = 4


def params(**kw):
    return pltpu.CompilerParams(vmem_limit_bytes=6 << 20, **kw)


def local_y(pos_y, tile_y, cells_y, total_y):
    return lax.rem(pos_y - tile_y * cells_y + total_y + total_y // 2, total_y) - total_y // 2


def smooth_z(block):
    near = pltpu.roll(block, 1, 1) + pltpu.roll(block, block.shape[1] - 1, 1)
    far = pltpu.roll(block, 2, 1) + pltpu.roll(block, block.shape[1] - 2, 1)
    return K0 * block + K1 * near + K2 * far


def split_dot(block, pick, dims):
    rows = block.shape[0]
    high = block.astype(BF16)
    low = (block - high.astype(F32)).astype(BF16)
    both = lax.dot_general(
        jnp.concatenate([high, low], axis=0), pick, (dims, ((), ())), preferred_element_type=F32
    )
    return both[:rows] + both[rows:]


def build_tables(pos_ref, pick_ref, here_ref, n, rec, tile_y, cells_y, total_y):
    depth, points = pick_ref.shape[1:]
    cell = lax.broadcasted_iota(I32, (depth, points), 0)
    pick_ref[n] = (cell == pos_ref[2, pl.ds(rec, 1), :]).astype(F32).astype(BF16)
    here_ref[pl.ds(n, 1), :] = local_y(pos_ref[1, pl.ds(rec, 1), :], tile_y, cells_y, total_y)


def weight_y(here_ref, n, cells_y):
    here = here_ref[pl.ds(n, 1), :]
    dist = jnp.abs(lax.broadcasted_iota(I32, (cells_y, here.shape[1]), 0) - here)
    return jnp.where(
        dist == 0, K0, jnp.where(dist == 1, K1, jnp.where(dist == 2, K2, 0.0))
    ).astype(F32)


def sample_group(size, field, plan_ref, pick_ref, here_ref, part_ref, group_at, count):
    _, comps, _, cells_y, _ = field.shape
    for k in range(size):
        n = jnp.minimum(size * group_at + k, count - 1)
        rec, hub = plan_ref[0, n], plan_ref[1, n]
        planes = [
            K0 * field[half, :, hub]
            + K1 * (field[half, :, hub - 1] + field[half, :, hub + 1])
            + K2 * (field[half, :, hub - 2] + field[half, :, hub + 2])
            for half in range(2)
        ]
        planes = [value.reshape(comps * cells_y, LANES) for value in planes]
        smooth = smooth_z(jnp.concatenate(planes, axis=1))
        inner = split_dot(smooth, pick_ref[n], ((1,), (0,)))
        value = jnp.sum(inner.reshape(comps, cells_y, -1) * weight_y(here_ref, n, cells_y)[None], axis=1)
        group, row = rec // 8, lax.rem(rec, 8)
        for half in range(2):
            for c in range(comps):
                part_ref[half * 8 + group, c, pl.ds(row, 1), :] = value[
                    c : c + 1, half * LANES : (half + 1) * LANES
                ]


def spread_group(size, field, plan_ref, pick_ref, here_ref, coef_ref, samp_ref, scale, group_at, count):
    _, comps, _, cells_y, _ = field.shape
    slabs = []
    for k in range(size):
        n = jnp.minimum(size * group_at + k, count - 1)
        rec, hub = plan_ref[0, n], plan_ref[1, n]
        factor = jnp.where(size * group_at + k < count, -scale, 0.0)
        group, row = rec // 8, lax.rem(rec, 8)
        sampled = [
            jnp.concatenate(
                [samp_ref[half * 8 + group, c, pl.ds(row, 1), :] for half in range(2)], axis=1
            )
            for c in range(comps)
        ]
        speed = jnp.sqrt(sampled[0] * sampled[0] + sampled[1] * sampled[1] + sampled[2] * sampled[2])
        strength = coef_ref[pl.ds(rec, 1), :] * speed * factor
        along = weight_y(here_ref, n, cells_y)
        weighted = jnp.concatenate([along * (strength * value) for value in sampled], axis=0)
        slab = smooth_z(split_dot(weighted, pick_ref[n], ((1,), (1,))))
        for half in range(2):
            part = slab[:, half * LANES : (half + 1) * LANES]
            slabs.append((half, hub, part.reshape(comps, cells_y, LANES)))
    for half, hub, slab in slabs:
        for d, weight in ((-2, K2), (-1, K1), (0, K0), (1, K1), (2, K2)):
            field[half, :, hub + d] += weight * slab


def make_plan(total_y, groups_y, pos_ref, tiles_ref, counts_ref, rows_ref, cells_x, cells_y):
    recs = pos_ref.shape[1]
    tile_x, tile_y = lax.axis_index("gx"), lax.axis_index("gy")
    rec = lax.broadcasted_iota(I32, (recs, LANES), 0)
    lane = lax.broadcasted_iota(I32, (recs, LANES), 1)
    square = lax.broadcasted_iota(I32, (recs, recs), 0) == lax.broadcasted_iota(I32, (recs, recs), 1)

    def column(row):
        return jnp.sum(jnp.where(square, row.astype(F32), 0.0), axis=1, keepdims=True).astype(I32)

    here = local_y(pos_ref[1], tile_y, cells_y, total_y)
    near = ((here >= -RAD) & (here < cells_y + RAD)).astype(I32)
    touched = jnp.max(near, axis=1, keepdims=True)
    hub = pos_ref[0, :, 0:1] - tile_x * cells_x
    first, number = column(tiles_ref[0:1, :]), column(tiles_ref[1:2, :])
    listed = lax.rem(tile_y - first + groups_y, groups_y) < number
    active = listed & (touched > 0) & (rec[:, 0:1] < counts_ref[0])
    big = jnp.int32(1 << 20)
    key = jnp.where(active, hub * recs + rec[:, 0:1], big)
    key_row = jnp.min(jnp.where(rec == lane, key, big), axis=0, keepdims=True)
    rank = jnp.sum((key_row < key).astype(F32), axis=1, keepdims=True).astype(I32)
    live = active.astype(F32)
    count = jnp.sum(live, axis=0, keepdims=True).astype(I32)
    mine = active & (rank == jnp.minimum(lane, count - 1))
    rows_ref[0:1, :] = jnp.sum(jnp.where(mine, rec, 0).astype(F32), axis=0, keepdims=True).astype(I32)
    rows_ref[1:2, :] = jnp.sum(jnp.where(mine, hub, 0).astype(F32), axis=0, keepdims=True).astype(I32)
    below = active & (hub < lane)
    rows_ref[2:3, :] = jnp.sum(below.astype(F32), axis=0, keepdims=True).astype(I32)


def over_records(count, step):
    full = count // GROUP
    pl.loop(0, full)(step(GROUP))
    pl.loop(full * (GROUP // SMALL), (count + SMALL - 1) // SMALL)(step(SMALL))


def sample_first(total_y, groups_y, vel_hbm, pos_hbm, tiles_hbm, counts_ref,
                 field, pos_ref, part_ref, plan_ref, pick_ref, here_ref, tiles_ref, rows_ref, sems):
    cells_x, cells_y = field.shape[2:4]
    tile_y = lax.axis_index("gy")
    chunk = cells_x // CHUNKS
    fetch_pos = pltpu.make_async_copy(pos_hbm, pos_ref, sems.at[2 * CHUNKS])
    fetch_tiles = pltpu.make_async_copy(tiles_hbm, tiles_ref, sems.at[2 * CHUNKS + 1])
    fetch_pos.start()
    fetch_tiles.start()

    def load(q, half):
        planes, lanes = pl.ds(q * chunk, chunk), pl.ds(half * LANES, LANES)
        return pltpu.make_async_copy(
            vel_hbm.at[:, planes, :, lanes], field.at[half, :, planes], sems.at[2 * q + half]
        )

    for q in range(CHUNKS):
        for half in range(2):
            load(q, half).start()
    part_ref[...] = jnp.zeros_like(part_ref)
    rows_ref[...] = jnp.zeros_like(rows_ref)
    fetch_pos.wait()
    fetch_tiles.wait()
    make_plan(total_y, groups_y, pos_ref, tiles_ref, counts_ref, rows_ref, cells_x, cells_y)
    fetch_plan = pltpu.make_async_copy(rows_ref, plan_ref, sems.at[2 * CHUNKS + 2])
    fetch_plan.start()
    fetch_plan.wait()
    count = plan_ref[2, LANES - 1]

    @pl.loop(0, count)
    def _(n):
        build_tables(pos_ref, pick_ref, here_ref, n, plan_ref[0, n], tile_y, cells_y, total_y)

    def sample(size):
        def body(at):
            sample_group(size, field, plan_ref, pick_ref, here_ref, part_ref, at, count)

        return body

    def ready(q, start):
        for half in range(2):
            load(q, half).wait()
        upto = jnp.where(q == CHUNKS - 1, count, plan_ref[2, (q + 1) * chunk - RAD])
        stop = upto // GROUP
        pl.loop(start, stop)(sample(GROUP))
        return stop

    full = lax.fori_loop(0, CHUNKS, ready, jnp.int32(0))
    pl.loop(full * (GROUP // SMALL), (count + SMALL - 1) // SMALL)(sample(SMALL))


def spread_and_sample(plan_ref, pick_ref, here_ref, coef_ref, samp_ref, _, field, part_ref):
    count = plan_ref[2, LANES - 1]
    part_ref[...] = jnp.zeros_like(part_ref)

    def spread(size):
        def body(at):
            spread_group(size, field, plan_ref, pick_ref, here_ref, coef_ref, samp_ref, TIME_STEP,
                         at, count)

        return body

    def sample(size):
        def body(at):
            sample_group(size, field, plan_ref, pick_ref, here_ref, part_ref, at, count)

        return body

    over_records(count, spread)
    over_records(count, sample)


def spread_last(plan_ref, pick_ref, here_ref, coef_ref, counts_ref, samp_a, samp_b, _,
                field, next_hbm, blade_hbm, blade, sems):
    comps, recs, _ = blade.shape
    chunk = field.shape[2] // CHUNKS
    count = plan_ref[2, LANES - 1]
    for half in range(2):
        lanes = pl.ds(half * LANES, LANES)
        for group in range(recs // 8):
            rows = pl.ds(group * 8, 8)
            a = [samp_a[half * 8 + group, c] for c in range(comps)]
            b = [samp_b[half * 8 + group, c] for c in range(comps)]
            speed_a = jnp.sqrt(a[0] * a[0] + a[1] * a[1] + a[2] * a[2])
            speed_b = jnp.sqrt(b[0] * b[0] + b[1] * b[1] + b[2] * b[2])
            rec = group * 8 + lax.broadcasted_iota(I32, (8, LANES), 0)
            strength = jnp.where(rec < counts_ref[0], coef_ref[rows, lanes] * -0.5, 0.0)
            for c in range(comps):
                blade[c, rows, lanes] = strength * (speed_a * a[c] + speed_b * b[c])
    put = pltpu.make_async_copy(blade, blade_hbm, sems.at[2 * CHUNKS])
    put.start()
    full = count // GROUP

    def spread(size):
        def body(at):
            spread_group(size, field, plan_ref, pick_ref, here_ref, coef_ref, samp_b,
                         0.5 * TIME_STEP, at, count)

        return body

    def store(q, half):
        planes, lanes = pl.ds(q * chunk, chunk), pl.ds(half * LANES, LANES)
        return pltpu.make_async_copy(
            field.at[half, :, planes], next_hbm.at[:, planes, :, lanes], sems.at[2 * q + half]
        )

    def finish(q, done):
        large, small = done
        upto = jnp.where(q == CHUNKS - 1, count, plan_ref[2, (q + 1) * chunk + RAD])
        large_stop = jnp.minimum((upto + GROUP - 1) // GROUP, full)
        small_stop = jnp.maximum((upto + SMALL - 1) // SMALL, small)
        pl.loop(large, large_stop)(spread(GROUP))
        pl.loop(small, small_stop)(spread(SMALL))
        for half in range(2):
            store(q, half).start()
        return large_stop, small_stop

    lax.fori_loop(0, CHUNKS, finish, (jnp.int32(0), full * (GROUP // SMALL)))
    for q in range(CHUNKS):
        for half in range(2):
            store(q, half).wait()
    put.wait()


def exchange(groups_x, groups_y, second, *refs):
    if second:
        old, refs = refs[0], refs[1:]
    (field, part_ref, inflow, result, samp_ref,
     y_send, y_recv, x_recv, gathered, mine, send_sem, recv_sem) = refs
    _, comps, cells_x, cells_y, _ = field.shape
    tile_x, tile_y = lax.axis_index("gx"), lax.axis_index("gy")
    last_x = groups_x - 1

    def peer(k):
        return lax.rem(tile_y + k, groups_y)

    north, south = peer(1), peer(groups_y - 1)
    barrier = pltpu.get_barrier_semaphore()
    for k in range(1, groups_y):
        pl.semaphore_signal(barrier, inc=1, device_id={"gy": peer(k)}, device_id_type=MESH)

    @pl.when(tile_x > 0)
    def _():
        pl.semaphore_signal(barrier, inc=1, device_id={"gx": tile_x - 1}, device_id_type=MESH)

    @pl.when(tile_x < last_x)
    def _():
        pl.semaphore_signal(barrier, inc=1, device_id={"gx": tile_x + 1}, device_id_type=MESH)

    @pl.loop(0, cells_x // 8)
    def _(block):
        rows = pl.ds(block * 8, 8)
        for c in range(comps):
            for half in range(2):
                y_send[0, half, c, rows, :] = field[half, c, rows, 0, :]
                y_send[1, half, c, rows, :] = field[half, c, rows, cells_y - 1, :]

    @pl.when(tile_x == 0)
    def _():
        for half in range(2):
            x_recv[0, half] = inflow[:, :, pl.ds(half * LANES, LANES)]

    @pl.when(tile_x == last_x)
    def _():
        x_recv[1] = field[:, :, cells_x - 1]

    neighbours = (tile_x > 0).astype(I32) + (tile_x < last_x).astype(I32)
    pl.semaphore_wait(barrier, groups_y - 1 + neighbours)

    def remote(src, dst, slot, where):
        return pltpu.make_async_remote_copy(
            src_ref=src, dst_ref=dst, send_sem=send_sem.at[slot], recv_sem=recv_sem.at[slot],
            device_id=where, device_id_type=MESH,
        )

    def part_copy(k):
        return remote(part_ref.at[peer(k)], gathered.at[k - 1], 0, {"gy": peer(k)})

    def sum_copy(k, owner):
        return remote(mine, samp_ref.at[owner], 1, {"gy": peer(k)})

    def every(sem):
        return pltpu.make_async_copy(gathered, gathered, sem)

    base = 1
    chunk = cells_x // CHUNKS

    def y_copy(q, side):
        rows = pl.ds(q * chunk, chunk)
        return remote(y_send.at[1 - side, :, :, rows, :], y_recv.at[side, :, :, rows, :],
                      2 * base + 2 + 2 * q + side, {"gy": south if side else north})

    to_east = remote(field.at[:, :, cells_x - 1], x_recv.at[0], 2 * base, {"gx": tile_x + 1})
    to_west = remote(field.at[:, :, 0], x_recv.at[1], 2 * base + 1, {"gx": tile_x - 1})

    for k in range(1, groups_y):
        part_copy(k).start()
    for q in range(CHUNKS - 1):
        for side in range(2):
            y_copy(q, side).start()

    @pl.when(tile_x < last_x)
    def _():
        to_east.start()

    @pl.when(tile_x > 0)
    def _():
        to_west.start()

    scale = 0.5 if second else 1.0
    a = scale * TIME_STEP * VISCOSITY
    b = scale * TIME_STEP * 0.5
    centre = scale * (1.0 - 6.0 * TIME_STEP * VISCOSITY)
    sub = lax.broadcasted_iota(I32, (8, LANES), 0)
    lane = lax.broadcasted_iota(I32, (8, LANES), 1)
    first_row, last_row = sub == 0, sub == 7
    first_lane, last_lane = lane == 0, lane == LANES - 1
    zero = jnp.zeros((8, LANES), F32)
    strips = cells_y // 8

    def tile(c, i, t, half):
        return field[half, c, i, pl.ds(8 * t, 8), :]

    def ghost(side, half, c, i):
        return y_recv[side, half, c, pl.ds(i, 8, stride=0), :]

    def plane(i, west, east):
        for t in range(strips):
            rows = pl.ds(8 * t, 8)
            here = [[tile(c, i, t, half) for half in range(2)] for c in range(comps)]
            lower, upper = [], []
            for c in range(comps):
                up = [pltpu.roll(v, 1, 1) for v in here[c]]
                down = [pltpu.roll(v, LANES - 1, 1) for v in here[c]]
                lower.append([jnp.where(first_lane, zero, up[0]), jnp.where(first_lane, up[0], up[1])])
                upper.append([jnp.where(last_lane, down[1], down[0]), jnp.where(last_lane, zero, down[1])])
            for half in range(2):
                bu, bv, bw = (b * here[c][half] for c in range(3))
                for c in range(comps):
                    value = here[c][half]
                    if t > 0:
                        to_s = field[half, c, i, pl.ds(8 * t - 1, 8), :]
                    else:
                        to_s = jnp.where(first_row, zero, pltpu.roll(value, 1, 0))
                    if t < strips - 1:
                        to_n = field[half, c, i, pl.ds(8 * t + 1, 8), :]
                    else:
                        to_n = jnp.where(last_row, zero, pltpu.roll(value, 7, 0))
                    out = (
                        centre * value
                        + ((a - bu) * east(half, c, rows) + (a + bu) * west(half, c, rows))
                        + ((a - bv) * to_n + (a + bv) * to_s)
                        + ((a - bw) * upper[c][half] + (a + bw) * lower[c][half])
                    )
                    if second:
                        out = out + 0.5 * old[half, c, i, rows, :]
                    result[half, c, i, rows, :] = out

    def inside(i):
        plane(
            i,
            lambda half, c, rows: field[half, c, i - 1, rows, :],
            lambda half, c, rows: field[half, c, i + 1, rows, :],
        )

    def piece(start, stop):
        @pl.loop(0, (stop - start) // STEP)
        def _(n):
            for k in range(STEP):
                inside(start + n * STEP + k)

    steps = (cells_x - 2) // STEP
    cuts = [1 + STEP * (steps * k // 4) for k in (0, 2, 4)]

    piece(cuts[0], cuts[1])
    every(recv_sem.at[0]).wait()
    total = functools.reduce(jnp.add, [gathered[k] for k in range(groups_y - 1)], part_ref[tile_y])
    mine[...] = total
    samp_ref[tile_y] = total
    for k in range(1, groups_y):
        sum_copy(k, tile_y).start()
    for q in (CHUNKS - 1,):
        for side in range(2):
            y_copy(q, side).start()
    piece(cuts[1], cuts[2])
    for i in range(cuts[2], cells_x - 1):
        inside(i)

    @pl.when(tile_x > 0)
    def _():
        to_east.wait_recv()

    @pl.when(tile_x < last_x)
    def _():
        to_west.wait_recv()

    plane(
        0,
        lambda half, c, rows: x_recv[0, half, c, rows, :],
        lambda half, c, rows: field[half, c, 1, rows, :],
    )
    plane(
        cells_x - 1,
        lambda half, c, rows: field[half, c, cells_x - 2, rows, :],
        lambda half, c, rows: x_recv[1, half, c, rows, :],
    )

    for q in range(CHUNKS):
        for side in range(2):
            y_copy(q, side).wait_recv()

        @pl.loop(0, chunk // STEP)
        def _(n):
            for k in range(STEP):
                i = q * chunk + n * STEP + k
                for side, t, mask in ((0, 0, first_row), (1, strips - 1, last_row)):
                    rows = pl.ds(8 * t, 8)
                    for half in range(2):
                        bv = b * tile(1, i, t, half)
                        weight = jnp.where(mask, a - bv if side else a + bv, 0.0)
                        for c in range(comps):
                            before = result[half, c, i, rows, :]
                            result[half, c, i, rows, :] = before + weight * ghost(side, half, c, i)

    every(recv_sem.at[1]).wait()
    every(send_sem.at[0]).wait()
    every(send_sem.at[1]).wait()
    for q in range(CHUNKS):
        for side in range(2):
            y_copy(q, side).wait_send()

    @pl.when(tile_x < last_x)
    def _():
        to_east.wait_send()

    @pl.when(tile_x > 0)
    def _():
        to_west.wait_send()


def local(groups_x, groups_y, velocity, inflow, positions, tiles, coefs, counts):
    comps, cells_x, cells_y, depth = velocity.shape
    total_y = cells_y * groups_y
    pos, tiles, coefs = positions[0].transpose(1, 0, 2), tiles[0].T, coefs[0]
    _, recs, points = pos.shape
    velocity, pos, tiles = (
        pltpu.with_memory_space_constraint(x, pltpu.HBM) for x in (velocity, pos, tiles)
    )
    grid = pltpu.VMEM((2, comps, cells_x, cells_y, LANES), F32)
    table = pltpu.VMEM((groups_y, comps, recs * points // (groups_y * LANES), LANES), F32)

    field, _, part, plan, picks, here = pl.pallas_call(
        functools.partial(sample_first, total_y, groups_y),
        out_shape=(
            grid,
            pltpu.VMEM(pos.shape, I32),
            table,
            pltpu.SMEM((8, LANES), I32),
            pltpu.VMEM((recs, depth, points), BF16),
            pltpu.VMEM((recs, points), I32),
        ),
        in_specs=[HBM, HBM, HBM, SMEM],
        out_specs=(VMEM, VMEM, VMEM, SMEM, VMEM, VMEM),
        scratch_shapes=[
            pltpu.VMEM(tiles.shape, I32),
            pltpu.VMEM((8, LANES), I32),
            pltpu.SemaphoreType.DMA((2 * CHUNKS + 3,)),
        ],
        compiler_params=params(),
        name="sample_first",
    )(velocity, pos, tiles, counts)

    def swap(second, *operands):
        sems = 4 + 2 * CHUNKS
        return pl.pallas_call(
            functools.partial(exchange, groups_x, groups_y, second),
            out_shape=(grid, table),
            in_specs=[VMEM] * len(operands),
            out_specs=(VMEM, VMEM),
            scratch_shapes=[
                pltpu.VMEM((2, 2, comps, cells_x, LANES), F32),
                pltpu.VMEM((2, 2, comps, cells_x, LANES), F32),
                pltpu.VMEM((2, 2, comps, cells_y, LANES), F32),
                pltpu.VMEM((groups_y - 1, *table.shape[1:]), F32),
                pltpu.VMEM(table.shape[1:], F32),
                pltpu.SemaphoreType.DMA((sems,)),
                pltpu.SemaphoreType.DMA((sems,)),
            ],
            compiler_params=params(collective_id=int(second), has_side_effects=True),
            name="exchange_second" if second else "exchange_first",
        )(*operands)

    section, samp_a = swap(False, field, part, inflow)
    section, part = pl.pallas_call(
        spread_and_sample,
        out_shape=(grid, table),
        in_specs=[SMEM] + [VMEM] * 5,
        out_specs=(VMEM, VMEM),
        input_output_aliases={5: 0},
        compiler_params=params(),
        name="spread_and_sample",
    )(plan, picks, here, coefs, samp_a, section)
    final, samp_b = swap(True, field, section, part, inflow)
    _, velocity_next, blade = pl.pallas_call(
        spread_last,
        out_shape=(
            grid,
            jax.ShapeDtypeStruct(velocity.shape, F32),
            jax.ShapeDtypeStruct(pos.shape, F32),
        ),
        in_specs=[SMEM, VMEM, VMEM, VMEM, SMEM, VMEM, VMEM, VMEM],
        out_specs=(VMEM, HBM, HBM),
        input_output_aliases={7: 0},
        scratch_shapes=[pltpu.VMEM(pos.shape, F32), pltpu.SemaphoreType.DMA((2 * CHUNKS + 1,))],
        compiler_params=params(),
        name="spread_last",
    )(plan, picks, here, coefs, counts, samp_a, samp_b, final)
    return (velocity_next, blade.transpose(1, 0, 2)[None])


def solution(mesh):
    return jax.shard_map(
        functools.partial(local, mesh.shape["gx"], mesh.shape["gy"]),
        mesh=mesh,
        in_specs=(
            P(None, "gx", "gy", None),
            P(None, "gy", None),
            P("gx", None, None, None),
            P("gx", None, None),
            P("gx", None, None),
            P("gx"),
        ),
        out_specs=(P(None, "gx", "gy", None), P("gx", None, None, None)),
        check_vma=False,
    )
```
